32 devices in a mesh: dp: 4 (over y, x), seq: 8 (over z, core).
Axes of the slice: x: 2, y: 2, z: 4, core: 2. Of those that a mesh axis runs over, the one named last changes fastest.
Arguments:
- tokens: bfloat16 [4, 4, 512, 1024], P('dp', None, 'seq'), may hold values from -6 to 6
- norm1_gain: bfloat16 [1024], P('dp'), may hold values from 0.5 to 1.5
- w_query: bfloat16 [1024, 1024], P('dp'), may hold values from -0.1875 to 0.1875
- w_latent: bfloat16 [1024, 512], P('dp'), may hold values from -0.1875 to 0.1875
- w_key_up: bfloat16 [256, 1024], P('dp'), may hold values from -0.375 to 0.375
- w_value_up: bfloat16 [256, 1024], P('dp'), may hold values from -0.375 to 0.375
- w_out: bfloat16 [1024, 1024], P('dp'), may hold values from -1.5 to 1.5
- norm2_gain: bfloat16 [1024], P('dp'), may hold values from 0.5 to 1.5
- w_gate: bfloat16 [1024, 2816], P('dp'), may hold values from -0.1875 to 0.1875
- w_up: bfloat16 [1024, 2816], P('dp'), may hold values from -0.1875 to 0.1875
- w_down: bfloat16 [2816, 1024], P('dp'), may hold values from -0.109375 to 0.109375
- out_grad: bfloat16 [4, 4, 512, 1024], P('dp', None, 'seq'), may hold values from -6 to 6
- seq_lengths: int32 [4, 66], P('dp'), may hold values from 0 to 1024, as said below
Outputs:
- layer_out: bfloat16 [4, 4, 512, 1024], P('dp', None, 'seq')
- tokens_grad: bfloat16 [4, 4, 512, 1024], P('dp', None, 'seq')
- norm1_gain_grad: float32 [1024], P('dp')
- w_query_grad: float32 [1024, 1024], P('dp')
- w_latent_grad: float32 [1024, 512], P('dp')
- w_key_up_grad: float32 [256, 1024], P('dp')
- w_value_up_grad: float32 [256, 1024], P('dp')
- w_out_grad: float32 [1024, 1024], P('dp')
- norm2_gain_grad: float32 [1024], P('dp')
- w_gate_grad: float32 [1024, 2816], P('dp')
- w_up_grad: float32 [1024, 2816], P('dp')
- w_down_grad: float32 [2816, 1024], P('dp')
The draws below stay inside these ranges and needn't reach their ends.
Inputs may be any that keep to these rules, and one draw needn't show every extreme that they name: `seq_lengths`: the entries of a stream sum to 2048. Even entries are sequence lengths; every stream holds one sequence of exactly 1024 positions. Odd entries are padding of at most 64 positions.
All inputs are finite; a program needn't handle non-finite values.
Results may differ from the reference program's by a relative error of at most 0.02.
Values may be sent and summed in bfloat16 or wider, within the bound.
No kernel may reach another device: no remote copies, remote signals or barrier semaphores. Data moves between devices by JAX's collectives and lax.ppermute only.
A program may use at most 256 MiB of HBM per device.

```python
import math
import jax
import jax.numpy as jnp
from jax import lax

D = 1024
HEADS = 16
HEAD_DIM = 64
GROUPS = 2
LATENT = 256
FF = 2816
BATCH = 4
SPAN = 512
MAXLEN = 1024
PIECES = 4
STREAM = 2048


def fill_region(base_key, region_total, pair_count):
    sub_keys = jax.random.split(base_key, 4)
    top_power = int(MAXLEN).bit_length() - 1
    powers = jax.random.randint(sub_keys[0], (BATCH, pair_count), 0, top_power + 1)
    lowest = jnp.left_shift(jnp.ones_like(powers), powers)
    extras = jax.random.randint(sub_keys[1], (BATCH, pair_count), 0, 1 << 30) % lowest
    wanted = jnp.minimum(lowest + extras, MAXLEN)
    even_slot = (jnp.arange(pair_count, dtype=jnp.int32) % 2 == 0)[None, :]
    wanted = jnp.where(even_slot, jnp.maximum(wanted, MAXLEN // 4), wanted)
    gap_on = (jax.random.randint(sub_keys[2], (BATCH, pair_count), 0, 4) == 0).astype(jnp.int32)
    gap_sizes = gap_on * jax.random.randint(sub_keys[3], (BATCH, pair_count), 1, MAXLEN // 16 + 1)
    stretch = jnp.stack([wanted, gap_sizes], axis=-1).reshape(BATCH, 2 * pair_count)
    run_ends = jnp.cumsum(stretch, axis=-1)
    return jnp.clip(region_total[:, None] - (run_ends - stretch), 0, stretch)


def stretch_table(base_key):
    pair_count = 8 * STREAM // MAXLEN
    sub_keys = jax.random.split(jax.random.fold_in(base_key, 11), 3)
    before_long = jax.random.randint(sub_keys[0], (BATCH,), 0, STREAM - MAXLEN + 1)
    first_part = fill_region(sub_keys[1], before_long, pair_count)
    second_part = fill_region(sub_keys[2], STREAM - MAXLEN - before_long, pair_count)
    middle_part = jnp.stack([jnp.full((BATCH,), MAXLEN, jnp.int32), jnp.zeros((BATCH,), jnp.int32)], axis=1)
    return jnp.concatenate([first_part, middle_part, second_part], axis=1).astype(jnp.int32)


def draw_seq_lengths(key, part):
    return stretch_table(key)


def steps_of(rng, extent, shards, smallest, top_value):
    loudness = 1.0
    for dim, blocks in shards:
        steps = jax.random.uniform(jax.random.fold_in(jax.random.fold_in(rng, 6), dim), (blocks,), jnp.float32, smallest / len(shards), top_value / len(shards))
        loudness = loudness * jnp.repeat(jnp.exp(steps), extent[dim] // blocks).reshape((-1,) + (1,) * (len(extent) - 1 - dim))
    return loudness


def gaussian(rng, shape, scale, most, cuts=(), held_as=jnp.bfloat16):
    level = steps_of(rng, shape, cuts, -0.22, 0.18) if cuts else 1.0
    values = jax.random.normal(rng, shape, jnp.float32) * scale * level
    return jnp.minimum(jnp.maximum(values, -most), most).astype(held_as)


def setup_inputs(seed: int = 0) -> dict:
    arg_keys = jax.random.split(jax.random.key(seed), 14)
    return {
        "tokens": gaussian(arg_keys[0], (BATCH, PIECES, SPAN, D), 1.0, 6.0, ((0, 4), (2, 8))),
        "norm1_gain": jnp.clip(1.0 + 0.1 * jax.random.normal(arg_keys[1], (D,), jnp.float32), 0.5, 1.5).astype(jnp.bfloat16),
        "w_query": gaussian(arg_keys[2], (D, HEADS * HEAD_DIM), D ** -0.5, 0.1875, ((0, 4),)),
        "w_latent": gaussian(arg_keys[3], (D, GROUPS * LATENT), D ** -0.5, 0.1875, ((0, 4),)),
        "w_key_up": gaussian(arg_keys[4], (LATENT, HEADS * HEAD_DIM), LATENT ** -0.5, 0.375, ((0, 4),)),
        "w_value_up": gaussian(arg_keys[5], (LATENT, HEADS * HEAD_DIM), LATENT ** -0.5, 0.375, ((0, 4),)),
        "w_out": gaussian(arg_keys[6], (HEADS * HEAD_DIM, D), 16 ** -0.5, 1.5, ((0, 4),)),
        "norm2_gain": jnp.clip(1.0 + 0.1 * jax.random.normal(arg_keys[7], (D,), jnp.float32), 0.5, 1.5).astype(jnp.bfloat16),
        "w_gate": gaussian(arg_keys[8], (D, FF), D ** -0.5, 0.1875, ((0, 4),)),
        "w_up": gaussian(arg_keys[9], (D, FF), D ** -0.5, 0.1875, ((0, 4),)),
        "w_down": gaussian(arg_keys[10], (FF, D), FF ** -0.5, 0.109375, ((0, 4),)),
        "out_grad": gaussian(arg_keys[11], (BATCH, PIECES, SPAN, D), 1.0, 6.0, ((0, 4), (2, 8))),
        "seq_lengths": draw_seq_lengths(jax.random.fold_in(arg_keys[13], 71), 0),
    }


@jax.custom_vjp
def low(v):
    return lax.optimization_barrier(v.astype(jnp.bfloat16)).astype(jnp.float32)

@jax.custom_vjp
def low_back(v):
    return v

def low_keep(v):
    return (low(v), None)

def low_pass(kept, grad):
    return (grad,)

def back_keep(v):
    return (v, None)

def back_low(kept, grad):
    return (low(grad),)
low.defvjp(low_keep, low_pass)
low_back.defvjp(back_keep, back_low)
NEG_FILL = -1e+30
NORM_EPS = 1e-05
HIGH_PREC = lax.Precision.HIGHEST

def rms_scale(values, gain):
    inverse = lax.rsqrt(lax.optimization_barrier(jnp.mean(values * values, axis=-1, keepdims=True)) + NORM_EPS)
    return values * inverse * gain

def seq_table(stretches):
    run_ends = jnp.cumsum(stretches).astype(jnp.int32)
    firsts = (run_ends - stretches).astype(jnp.int32)
    return (firsts[0::2], stretches[0::2].astype(jnp.int32))

def label_rows(starts, lengths, positions):
    inside = (positions[:, None] >= starts[None, :]) & (positions[:, None] < starts[None, :] + lengths[None, :])
    labels = jnp.arange(1, starts.shape[0] + 1, dtype=jnp.int32)
    return lax.optimization_barrier(jnp.sum(jnp.where(inside, labels[None, :], 0), axis=1)).astype(jnp.int32)

def stream_attention(absorbed, latent, stretches):
    stream_len = latent.shape[0]
    block_rows = math.gcd(stream_len, 512)
    window = MAXLEN + block_rows
    per_group = HEADS // GROUPS
    score_scale = 1.0 / math.sqrt(HEAD_DIM)
    positions = jnp.arange(stream_len, dtype=jnp.int32)
    starts, lengths = seq_table(stretches)
    labels = label_rows(starts, lengths, positions)
    padded_latent = jnp.concatenate([jnp.zeros((MAXLEN, latent.shape[1]), jnp.float32), latent], axis=0)
    padded_labels = jnp.concatenate([jnp.full((MAXLEN,), -1, jnp.int32), labels])

    def one_block(block_id):
        first_row = (block_id * block_rows).astype(jnp.int32)
        row_vals = lax.dynamic_slice_in_dim(absorbed, first_row, block_rows, 0)
        row_labels = lax.dynamic_slice_in_dim(labels, first_row, block_rows, 0)
        key_vals = lax.dynamic_slice_in_dim(padded_latent, first_row, window, 0)
        key_labels = lax.dynamic_slice_in_dim(padded_labels, first_row, window, 0)
        row_pos = first_row + jnp.arange(block_rows, dtype=jnp.int32)
        key_pos = first_row - MAXLEN + jnp.arange(window, dtype=jnp.int32)
        same_seq = (row_labels[:, None] == key_labels[None, :]) & (row_labels[:, None] > 0) & (key_pos[None, :] <= row_pos[:, None])
        allowed = same_seq | (key_pos[None, :] == row_pos[:, None])
        outputs = []
        for group_id in range(GROUPS):
            group_queries = row_vals[:, group_id * per_group:(group_id + 1) * per_group, :]
            group_keys = key_vals[:, group_id * LATENT:(group_id + 1) * LATENT]
            scores = jnp.einsum('thc,kc->thk', group_queries, group_keys, precision=HIGH_PREC) * score_scale
            scores = low_back(scores)
            scores = jnp.where(allowed[:, None, :], scores, NEG_FILL)
            row_top = lax.optimization_barrier(jnp.max(scores, axis=-1, keepdims=True))
            expo_vals = jnp.exp(scores - row_top)
            prob_vals = low(expo_vals / lax.optimization_barrier(jnp.sum(expo_vals, axis=-1, keepdims=True)))
            outputs.append(jnp.einsum('thk,kc->thc', prob_vals, group_keys, precision=HIGH_PREC))
        return jnp.concatenate(outputs, axis=1)
    mixed = lax.map(jax.checkpoint(one_block), jnp.arange(stream_len // block_rows, dtype=jnp.int32))
    return mixed.reshape(stream_len, HEADS, LATENT)

def forward(values, seq_lengths):
    tokens_in, norm1_gain, w_query, w_latent, w_key_up, w_value_up, w_out, norm2_gain, w_gate, w_up, w_down = values
    batch_count = tokens_in.shape[0]
    row_width = tokens_in.shape[-1]
    tokens = tokens_in.reshape(batch_count, -1, row_width)
    stream_len = tokens.shape[1]
    normed = low(rms_scale(tokens, norm1_gain))
    queries = low(low_back(jnp.einsum('btd,de->bte', normed, w_query, precision=HIGH_PREC)))
    latent = low(low_back(jnp.einsum('btd,de->bte', normed, w_latent, precision=HIGH_PREC)))
    key_up = w_key_up.reshape(LATENT, HEADS, HEAD_DIM)
    value_up = w_value_up.reshape(LATENT, HEADS, HEAD_DIM)
    query_heads = queries.reshape(batch_count, stream_len, HEADS, HEAD_DIM)
    absorbed = low(low_back(jnp.einsum('bthd,chd->bthc', query_heads, key_up, precision=HIGH_PREC)))

    def per_stream(stream_items):
        return stream_attention(stream_items[0], stream_items[1], stream_items[2])
    mixed = lax.map(per_stream, (absorbed, latent, seq_lengths))
    mixed_round = low(low_back(mixed))
    heads_out = jnp.einsum('bthc,chd->bthd', mixed_round, value_up, precision=HIGH_PREC)
    heads_out = low(low_back(heads_out.reshape(batch_count, stream_len, HEADS * HEAD_DIM)))
    resid = tokens + low_back(jnp.einsum('bte,ed->btd', heads_out, w_out, precision=HIGH_PREC))
    normed_two = low(rms_scale(resid, norm2_gain))
    gate_vals = low_back(jnp.einsum('btd,df->btf', normed_two, w_gate, precision=HIGH_PREC))
    up_vals = low_back(jnp.einsum('btd,df->btf', normed_two, w_up, precision=HIGH_PREC))
    hidden = low(gate_vals * jax.nn.sigmoid(gate_vals) * up_vals)
    result = resid + low_back(jnp.einsum('btf,fd->btd', hidden, w_down, precision=HIGH_PREC))
    return result.reshape(tokens_in.shape)

def reference(tokens, norm1_gain, w_query, w_latent, w_key_up, w_value_up, w_out, norm2_gain, w_gate, w_up, w_down, out_grad, seq_lengths):
    floats = tuple((item_val.astype(jnp.float32) for item_val in (tokens, norm1_gain, w_query, w_latent, w_key_up, w_value_up, w_out, norm2_gain, w_gate, w_up, w_down)))

    def layer_run(*values):
        return forward(values, seq_lengths)
    result, pull_back = jax.vjp(layer_run, *floats)
    grads = pull_back(out_grad.astype(jnp.float32))
    return (result.astype(jnp.bfloat16), grads[0].astype(jnp.bfloat16), grads[1], grads[2], grads[3], grads[4], grads[5], grads[6], grads[7], grads[8], grads[9], grads[10])
```

```python
import functools
import math

import jax
import jax.numpy as jnp
from jax import lax
from jax.experimental import pallas as pl
from jax.experimental.pallas import tpu as pltpu
from jax.sharding import Mesh
from jax.sharding import PartitionSpec as P

HEADS = 16
HEAD_DIM = 64
GROUPS = 2
LATENT = 256
PER_GROUP = HEADS // GROUPS
GROUP_COLS = PER_GROUP * HEAD_DIM
KEY_BLOCK = 256
SCALE = 1.0 / math.sqrt(HEAD_DIM)
NEG_FILL = -1e30
NORM_EPS = 1e-05
F32 = jnp.float32
BF16 = jnp.bfloat16
DP = "dp"
SEQ = ("z", "core")
CHIP = ("dp", "core")


def mm(a, b):
    return jnp.dot(a, b, preferred_element_type=F32)


def mm_nt(a, b):
    return lax.dot_general(a, b, (((1,), (1,)), ((), ())), preferred_element_type=F32)


def mm_tn(a, b):
    return lax.dot_general(a, b, (((0,), (0,)), ((), ())), preferred_element_type=F32)


def low_lanes(rows):
    return lax.broadcasted_iota(jnp.int32, (rows, 2 * HEAD_DIM), 1) < HEAD_DIM


def pair_cols(pair):
    return slice(2 * HEAD_DIM * pair, 2 * HEAD_DIM * (pair + 1))


def expand_heads(vals, up_proj):
    low = low_lanes(vals.shape[0])
    out = []
    for pair in range(PER_GROUP // 2):
        part = vals[:, pair_cols(pair)]
        proj = up_proj[:, pair_cols(pair)]
        zero = jnp.zeros_like(part)
        out.append(mm_nt(jnp.where(low, part, zero), proj))
        out.append(mm_nt(jnp.where(low, zero, part), proj))
    return out


def shrink_heads(parts, up_proj):
    low = low_lanes(parts[0].shape[0])
    out = []
    for pair in range(PER_GROUP // 2):
        proj = up_proj[:, pair_cols(pair)]
        out.append(jnp.where(low, mm(parts[2 * pair], proj), mm(parts[2 * pair + 1], proj)))
    return jnp.concatenate(out, axis=1)


def outer_heads(parts, vals):
    low = low_lanes(LATENT)
    out = []
    for pair in range(PER_GROUP // 2):
        part = vals[:, pair_cols(pair)]
        out.append(jnp.where(low, mm_tn(parts[2 * pair], part), mm_tn(parts[2 * pair + 1], part)))
    return jnp.concatenate(out, axis=1)


def load_keys(lat_ref, slot_ref, block, strips, per_piece):
    piece = block // per_piece
    first = (block - piece * per_piece) * strips
    parts = [lat_ref[slot_ref[first + i], piece] for i in range(strips)]
    return jnp.concatenate(parts, axis=0), piece, first


def visible(block, base, starts, rows):
    row_pos = base + lax.broadcasted_iota(jnp.int32, (rows, KEY_BLOCK), 0)
    key_pos = block * KEY_BLOCK + lax.broadcasted_iota(jnp.int32, (rows, KEY_BLOCK), 1)
    return (key_pos >= starts) & (key_pos <= row_pos)


def masked(scores, seen, rows):
    tall = scores.shape[0]
    split = scores.reshape(PER_GROUP, rows, KEY_BLOCK)
    return jnp.where(seen[None], split, NEG_FILL).reshape(tall, KEY_BLOCK)


def forward_body(
    first_piece, lo_ref, hi_ref, base_ref, slot_ref, start_ref, lat_ref, query_ref, key_up_ref, value_up_ref,
    abs_ref, mixed_ref, lse_ref, out_ref, top_ref, sum_ref, acc_ref,
):
    piece_id = pl.program_id(1) + first_piece
    nseq, _, strip, _ = lat_ref.shape
    rows = query_ref.shape[0]
    strips = KEY_BLOCK // strip
    per_piece = nseq // strips
    for head, part in enumerate(expand_heads(query_ref[...], key_up_ref[...])):
        abs_ref[0, 0, head] = part.astype(BF16) * jnp.asarray(SCALE, BF16)
    tall = PER_GROUP * rows
    top_ref[...] = jnp.full(top_ref.shape, NEG_FILL, F32)
    sum_ref[...] = jnp.zeros(sum_ref.shape, F32)
    acc_ref[...] = jnp.zeros(acc_ref.shape, F32)
    starts = jnp.broadcast_to(start_ref[0][:, 0:1], (rows, KEY_BLOCK))

    def step(block, carry):
        keys, _, _ = load_keys(lat_ref, slot_ref, block, strips, per_piece)
        seen = visible(block, base_ref[piece_id], starts, rows)
        scores = masked(mm_nt(abs_ref[0, 0].reshape(tall, LATENT), keys), seen, rows)
        old_top = top_ref[...]
        new_top = jnp.maximum(old_top, jnp.max(scores, axis=1, keepdims=True))
        shrink = jnp.exp(old_top - new_top)
        probs = jnp.exp(scores - new_top)
        top_ref[...] = new_top
        sum_ref[...] = sum_ref[...] * shrink + jnp.sum(probs, axis=1, keepdims=True)
        acc_ref[...] = acc_ref[...] * shrink + mm(probs.astype(BF16), keys)
        return carry

    lax.fori_loop(lo_ref[piece_id], hi_ref[piece_id], step, 0)
    total = sum_ref[...]
    lse_ref[0, 0] = jnp.broadcast_to(top_ref[...] + jnp.log(total), (tall, 128))
    mixed = (acc_ref[...] * (1.0 / total)).astype(BF16).reshape(PER_GROUP, rows, LATENT)
    mixed_ref[0, 0] = mixed
    out_ref[...] = shrink_heads([mixed[h] for h in range(PER_GROUP)], value_up_ref[...]).astype(BF16)


def backward_body(
    first_piece, carried, *refs,
):
    refs = list(refs)
    lo_ref, hi_ref, base_ref, slot_ref, start_ref, lat_ref, query_ref, key_up_ref, value_up_ref = refs[:9]
    abs_ref, mixed_ref, lse_ref, grad_ref = refs[9:13]
    rest = refs[13:]
    if carried:
        carry_ref, dquery_ref, dlat_ref, key_grad_ref, value_grad_ref = rest[:5]
    else:
        dquery_ref, dlat_ref, carry_ref, key_grad_ref, value_grad_ref = rest[:5]
    dmix_ref, delta_ref, acc_ref, dkey_ref = rest[5:]
    step_id = pl.program_id(1)
    piece_id = step_id + first_piece
    nseq, _, strip, _ = lat_ref.shape
    rows = query_ref.shape[0]
    strips = KEY_BLOCK // strip
    per_piece = nseq // strips
    tall = PER_GROUP * rows

    @pl.when(step_id == 0)
    def _():
        if carried:
            dkey_ref[...] = carry_ref[...]
        else:
            dkey_ref[...] = jnp.zeros(dkey_ref.shape, F32)
        key_grad_ref[...] = jnp.zeros(key_grad_ref.shape, F32)
        value_grad_ref[...] = jnp.zeros(value_grad_ref.shape, F32)

    grads = grad_ref[...]
    for head, part in enumerate(expand_heads(grads, value_up_ref[...])):
        dmix_ref[head] = part.astype(BF16)
    value_grad_ref[...] += outer_heads([mixed_ref[0, 0, h] for h in range(PER_GROUP)], grads)
    dmix_all = dmix_ref[...].reshape(tall, LATENT).astype(F32)
    mixed_all = mixed_ref[0, 0].reshape(tall, LATENT).astype(F32)
    delta_ref[...] = jnp.sum(dmix_all * mixed_all, axis=1, keepdims=True)
    acc_ref[...] = jnp.zeros(acc_ref.shape, F32)
    starts = jnp.broadcast_to(start_ref[0][:, 0:1], (rows, KEY_BLOCK))

    def step(block, carry):
        keys, key_piece, first = load_keys(lat_ref, slot_ref, block, strips, per_piece)
        seen = visible(block, base_ref[piece_id], starts, rows)
        absorbed = abs_ref[0, 0].reshape(tall, LATENT)
        dmix = dmix_ref[...].reshape(tall, LATENT)
        probs = jnp.exp(masked(mm_nt(absorbed, keys) - lse_ref[0, 0][:, 0:1], seen, rows))
        d_scores = (probs * (mm_nt(dmix, keys) - delta_ref[...])).astype(BF16)
        acc_ref[...] += mm(d_scores, keys)
        d_keys = mm_tn(d_scores, absorbed) + mm_tn(probs.astype(BF16), dmix)
        for i in range(strips):
            dkey_ref[slot_ref[first + i], key_piece] += d_keys[i * strip : (i + 1) * strip]
        return carry

    lax.fori_loop(lo_ref[piece_id], hi_ref[piece_id], step, 0)
    d_abs = (acc_ref[...] * SCALE).astype(BF16).reshape(PER_GROUP, rows, LATENT)
    parts = [d_abs[h] for h in range(PER_GROUP)]
    dquery_ref[...] = shrink_heads(parts, key_up_ref[...]).astype(BF16)
    key_grad_ref[...] += outer_heads(parts, query_ref[...])

    @pl.when(step_id == pl.num_programs(1) - 1)
    def _():
        if carried:
            dlat_ref[...] = dkey_ref[...].astype(BF16)
        else:
            dlat_ref[...] = dkey_ref[:, first_piece:].astype(BF16)
            carry_ref[...] = dkey_ref[:, :first_piece]


def attention_specs(nseq, strip, first_piece):
    tall = PER_GROUP * strip

    def lat(pieces):
        return pl.BlockSpec((nseq, pieces, strip, LATENT), lambda g, p, *_: (0, 0, 0, g))

    table = pl.BlockSpec((1, strip, 128), lambda g, p, *_: (p + first_piece, 0, 0))
    rows = pl.BlockSpec((strip, GROUP_COLS), lambda g, p, *_: (p + first_piece, g))
    mine = pl.BlockSpec((strip, GROUP_COLS), lambda g, p, *_: (p, g))
    proj = pl.BlockSpec((LATENT, GROUP_COLS), lambda g, p, *_: (0, g))
    heads = pl.BlockSpec((1, 1, PER_GROUP, strip, LATENT), lambda g, p, *_: (g, p, 0, 0, 0))
    lse = pl.BlockSpec((1, 1, tall, 128), lambda g, p, *_: (g, p, 0, 0))
    return table, lat, rows, mine, proj, heads, lse


def kernel_params():
    return pltpu.CompilerParams(dimension_semantics=("arbitrary", "arbitrary"), vmem_limit_bytes=56 << 20)


def attention_cost(nseq, pieces, strip, matmuls):
    pairs = HEADS * pieces * strip * nseq * strip * 2
    return pl.CostEstimate(
        flops=2 * matmuls * pairs * LATENT, transcendentals=pairs, bytes_accessed=32 << 20
    )


def attention_forward(first_piece, pieces, tables, table, latents, queries, key_up, value_up):
    nseq, all_pieces, strip, _ = latents.shape
    tall = PER_GROUP * strip
    t_spec, lat_spec, row_spec, mine_spec, proj_spec, head_spec, lse_spec = attention_specs(nseq, strip, first_piece)
    head_shape = jax.ShapeDtypeStruct((GROUPS, pieces, PER_GROUP, strip, LATENT), BF16)
    return pl.pallas_call(
        functools.partial(forward_body, first_piece),
        name="attention_forward",
        grid_spec=pltpu.PrefetchScalarGridSpec(
            num_scalar_prefetch=len(tables),
            grid=(GROUPS, pieces),
            in_specs=[t_spec, lat_spec(all_pieces), row_spec, proj_spec, proj_spec],
            out_specs=[head_spec, head_spec, lse_spec, mine_spec],
            scratch_shapes=[
                pltpu.VMEM((tall, 1), F32),
                pltpu.VMEM((tall, 1), F32),
                pltpu.VMEM((tall, LATENT), F32),
            ],
        ),
        out_shape=[
            head_shape,
            head_shape,
            jax.ShapeDtypeStruct((GROUPS, pieces, tall, 128), F32),
            jax.ShapeDtypeStruct((pieces * strip, queries.shape[1]), BF16),
        ],
        compiler_params=kernel_params(),
        cost_estimate=attention_cost(nseq, pieces, strip, 2),
    )(*tables, table, latents, queries, key_up, value_up)


def attention_backward(
    first_piece, pieces, tables, table, latents, queries, key_up, value_up, absorbed, mixed, lse, grads, carry
):
    nseq, all_pieces, strip, lat_width = latents.shape
    tall = PER_GROUP * strip
    carried = carry is not None
    t_spec, lat_spec, row_spec, mine_spec, proj_spec, head_spec, lse_spec = attention_specs(nseq, strip, first_piece)
    seen_pieces = pieces if carried else all_pieces
    in_specs = [
        t_spec, lat_spec(all_pieces), row_spec, proj_spec, proj_spec, head_spec, head_spec, lse_spec, mine_spec,
    ]
    operands = [table, latents, queries, key_up, value_up, absorbed, mixed, lse, grads]
    out_specs = [mine_spec, lat_spec(pieces)]
    out_shape = [
        jax.ShapeDtypeStruct((pieces * strip, queries.shape[1]), BF16),
        jax.ShapeDtypeStruct((nseq, pieces, strip, lat_width), BF16),
    ]
    if carried:
        in_specs.append(lat_spec(pieces))
        operands.append(carry)
    else:
        out_specs.append(lat_spec(first_piece))
        out_shape.append(jax.ShapeDtypeStruct((nseq, first_piece, strip, lat_width), F32))
    proj_shape = jax.ShapeDtypeStruct(key_up.shape, F32)
    return pl.pallas_call(
        functools.partial(backward_body, first_piece, carried),
        name="attention_backward",
        grid_spec=pltpu.PrefetchScalarGridSpec(
            num_scalar_prefetch=len(tables),
            grid=(GROUPS, pieces),
            in_specs=in_specs,
            out_specs=[*out_specs, proj_spec, proj_spec],
            scratch_shapes=[
                pltpu.VMEM((PER_GROUP, strip, LATENT), BF16),
                pltpu.VMEM((tall, 1), F32),
                pltpu.VMEM((tall, LATENT), F32),
                pltpu.VMEM((nseq, seen_pieces, strip, LATENT), F32),
            ],
        ),
        out_shape=[*out_shape, proj_shape, proj_shape],
        compiler_params=kernel_params(),
        cost_estimate=attention_cost(nseq, pieces, strip, 5),
    )(*tables, *operands)


def row_starts(stretches, positions):
    entry = jnp.arange(stretches.shape[0], dtype=jnp.int32)
    ends = jnp.sum(jnp.where(entry[None, :] <= entry[:, None], stretches[None, :], 0), axis=1)
    firsts = (ends - stretches)[0::2]
    ends = ends[0::2]
    inside = (positions[:, None] >= firsts[None, :]) & (positions[:, None] < ends[None, :])
    first = jnp.sum(jnp.where(inside, firsts[None, :], 0), axis=1)
    return jnp.where(jnp.any(inside, axis=1), first, positions)


def inverse_rms(values):
    return lax.rsqrt(jnp.mean(values * values, axis=-1, keepdims=True) + NORM_EPS)


def norm_pull(values, inverse, gain, grads):
    scaled = gain * grads
    return inverse * scaled - values * (inverse**3) * jnp.mean(scaled * values, axis=-1, keepdims=True)


def my_half(shard):
    half = shard.shape[0] // 2
    return lax.dynamic_slice_in_dim(shard, lax.axis_index("core") * half, half, 0)


def swap_core(x):
    return lax.ppermute(x, "core", [(0, 1), (1, 0)])


def partner(x, step):
    return lax.ppermute(x, DP, [(i, i ^ step) for i in range(lax.axis_size(DP))])


def from_behind(x, step):
    nz = lax.axis_size("z")
    return lax.ppermute(x, "z", [(i, (i + step) % nz) for i in range(nz)])


def from_ahead(x, step):
    nz = lax.axis_size("z")
    return lax.ppermute(x, "z", [((i + step) % nz, i) for i in range(nz)])


def gather_dp(x):
    return [x] + [partner(x, step) for step in range(1, lax.axis_size(DP))]


def scatter_dp(parts):
    total = parts[0].astype(F32)
    for step in range(1, len(parts)):
        total = total + partner(parts[step].astype(BF16), step).astype(F32)
    return total


def after(x, *others):
    return lax.optimization_barrier((x, *others))[0]


def per_device(
    tokens, norm1_gain, w_query, w_latent, w_key_up, w_value_up, w_out, norm2_gain,
    w_gate, w_up, w_down, out_grad, seq_lengths,
):
    ndp = lax.axis_size(DP)
    nz = lax.axis_size("z")
    nseq = 2 * nz
    pieces, strip, width = tokens.shape[1:]
    span = strip * nseq
    rows = pieces * strip
    lat_width = GROUPS * LATENT
    my_z, my_core, my_dp = lax.axis_index("z"), lax.axis_index("core"), lax.axis_index(DP)
    my_seq = my_z * 2 + my_core
    shard = norm1_gain.shape[0]
    slice_ff = w_down.shape[0]
    wide_ff = -(-slice_ff // 128) * 128
    half = shard // 2

    gains = jnp.pad(jnp.concatenate([norm1_gain, norm2_gain])[None, :], ((0, 15), (0, lat_width - 2 * shard)))
    own_head = jnp.concatenate([my_half(w_latent), gains], axis=0)
    by_step = jnp.stack(gather_dp(own_head))
    other = swap_core(by_step)
    core_pair = jnp.where(my_core == 0, jnp.stack([by_step, other]), jnp.stack([other, by_step]))
    order = jnp.arange(ndp, dtype=jnp.int32) ^ my_dp
    head_pack = jnp.stack([lax.dynamic_index_in_dim(core_pair, order[i], 1, False) for i in range(ndp)])
    latent_w = head_pack[:, :, :half].reshape(width, lat_width)
    gains = head_pack[:, 0, half].astype(F32)
    gain_one = gains[:, :shard].reshape(1, width)
    gain_two = gains[:, shard : 2 * shard].reshape(1, width)
    pack = lax.all_gather(
        jnp.concatenate([my_half(w_query), my_half(w_key_up), my_half(w_value_up), my_half(w_out)], axis=0),
        CHIP,
        axis=0,
    )
    up_half = w_key_up.shape[0] // 2
    cuts = [0, half, half + up_half, half + 2 * up_half, 2 * half + 2 * up_half]
    query_w, key_w, value_w, out_w = (
        pack[:, a:b].reshape(-1, width) for a, b in zip(cuts[:-1], cuts[1:])
    )

    piece_base = jnp.arange(pieces, dtype=jnp.int32) * span + my_seq * strip
    row_pos = piece_base[:, None] + jnp.arange(strip, dtype=jnp.int32)[None, :]
    starts = row_starts(seq_lengths[0], row_pos.reshape(-1)).reshape(pieces, strip)
    seq_ids = jnp.arange(nseq, dtype=jnp.int32)
    slots = (seq_ids % 2 ^ my_core) * nz + (my_z - seq_ids // 2) % nz
    tables = (
        starts[:, 0] // KEY_BLOCK, (piece_base + strip + KEY_BLOCK - 1) // KEY_BLOCK, piece_base, slots,
    )
    table = jnp.broadcast_to(starts[:, :, None], (pieces, strip, 128))

    tok = tokens[0].reshape(rows, width).astype(F32)
    inv_one = inverse_rms(tok)
    normed = (tok * inv_one * gain_one).astype(BF16)
    latent = mm(normed, latent_w).astype(BF16).reshape(pieces, strip, lat_width)
    core_lat = jnp.stack([latent] + [from_behind(latent, step) for step in range(1, nz)])
    latents = jnp.concatenate([core_lat, swap_core(core_lat)], axis=0)
    queries = mm(normed, query_w).astype(BF16)

    def column_slices(w):
        parts = w.reshape(shard, ndp, slice_ff).transpose(1, 0, 2)
        return jnp.pad(parts, ((0, 0), (0, 0), (0, wide_ff - slice_ff)))

    sliced = jnp.stack([column_slices(w_gate), column_slices(w_up)], axis=1)
    sliced = lax.all_to_all(after(sliced, queries), DP, 0, 0, tiled=True)
    gate_w = sliced[:, 0].reshape(width, wide_ff)
    up_w = sliced[:, 1].reshape(width, wide_ff)
    down_w = jnp.pad(w_down, ((0, wide_ff - slice_ff), (0, 0)))

    grad_rows = out_grad[0].reshape(rows, width)
    grad_blocks = lax.all_gather(after(grad_rows, pack), DP, axis=0)
    grad_blocks = [lax.dynamic_index_in_dim(grad_blocks, order[i], 0, False) for i in range(ndp)]
    cut = pieces // 2
    chunks = [(cut, pieces - cut), (0, cut)]

    def rows_of(x, chunk):
        return x[chunk[0] * strip : (chunk[0] + chunk[1]) * strip]

    kept = []
    turn = queries
    for chunk in chunks:
        absorbed, mixed, lse, heads_out = attention_forward(
            *chunk, tables, table, latents, after(queries, turn), key_w, value_w
        )
        resid = rows_of(tok, chunk) + mm(heads_out, out_w)
        inv_two = inverse_rms(resid)
        normed_two = (resid * inv_two * gain_two).astype(BF16)
        kept.append((absorbed, mixed, lse, heads_out, resid, inv_two, gather_dp(normed_two)))
        turn = normed_two

    ff_state = []
    d_resids = []
    for chunk, state in zip(chunks, kept):
        size = chunk[1] * strip
        resid, inv_two, blocks = state[4:]
        normed_all = after(jnp.concatenate(blocks), turn)
        grad_all = jnp.concatenate([rows_of(x, chunk) for x in grad_blocks])
        gate = mm(normed_all, gate_w)
        up = mm(normed_all, up_w)
        sig = 1.0 / (1.0 + jnp.exp(-gate))
        silu = gate * sig
        hidden = (silu * up).astype(BF16)
        d_hidden = mm_nt(grad_all, down_w)
        d_gate = (d_hidden * up * (sig * (1.0 + gate * (1.0 - sig)))).astype(BF16)
        d_up = (d_hidden * silu).astype(BF16)
        d_part = (mm_nt(d_gate, gate_w) + mm_nt(d_up, up_w)).astype(BF16)
        turn = d_part
        d_normed_two = scatter_dp([d_part[i * size : (i + 1) * size] for i in range(ndp)])
        d_resids.append(
            rows_of(grad_rows, chunk).astype(F32) + norm_pull(resid, inv_two, gain_two, d_normed_two)
        )
        ff_state.append((normed_all, grad_all, hidden, d_gate, d_up))

    normed_all, grad_all, hidden, d_gate, d_up = (jnp.concatenate(parts) for parts in zip(*ff_state))
    down_grad = mm_tn(hidden, grad_all)[:slice_ff].astype(BF16)
    out_part = mm(hidden, down_w).astype(BF16)

    def tiles(x):
        *lead, a, b = x.shape
        x = x.reshape(*lead, a // 8, 8, b // 128, 128)
        return jnp.swapaxes(x, -2, -3).reshape(*lead, a * b // 1024, 8, 128)

    def untiled(x, a, b):
        lead = x.shape[:-3]
        x = x.reshape(*lead, a // 8, b // 128, 8, 128)
        return jnp.swapaxes(x, -2, -3).reshape(*lead, a, b)

    down_rows = -(-slice_ff // (8 * nseq)) * 8
    own_rows = -(-shard // (8 * nseq)) * 8

    def by_owner(grad):
        parts = grad.astype(BF16).reshape(ndp, shard, wide_ff)
        parts = jnp.pad(parts, ((0, 0), (0, own_rows * nseq - shard), (0, 0)))
        parts = parts.reshape(ndp, nseq, own_rows, wide_ff).transpose(1, 0, 2, 3)
        return tiles(parts.reshape(nseq, ndp * own_rows, wide_ff))

    ff_pack = jnp.concatenate(
        [
            tiles(jnp.pad(down_grad, ((0, down_rows * nseq - slice_ff), (0, 0))).reshape(nseq, down_rows, width)),
            by_owner(mm_tn(normed_all, d_gate)),
            by_owner(mm_tn(normed_all, d_up)),
        ],
        axis=1,
    )
    turn = ff_pack
    ff_pack = lax.psum_scatter(ff_pack, SEQ, scatter_dimension=0, tiled=True)[0]
    ff_reduced = ff_pack
    down_tiles = down_rows * width // 1024
    each = own_rows * wide_ff // 1024
    swap = ff_pack[down_tiles:].reshape(2, ndp, each, 8, 128)
    swap = lax.all_to_all(swap, DP, 1, 1, tiled=True)
    ff_pack = jnp.concatenate([ff_pack[:down_tiles], swap.reshape(2 * ndp * each, 8, 128)], axis=0)
    ff_pack = lax.all_gather(ff_pack, SEQ, axis=0)
    down_out = untiled(ff_pack[:, :down_tiles], down_rows, width).reshape(-1, width)[:slice_ff].astype(F32)
    halves = ff_pack[:, down_tiles:].reshape(nseq, 2, ndp, each, 8, 128)

    def joined(which):
        x = untiled(halves[:, which], own_rows, wide_ff)[..., :slice_ff]
        return x.transpose(0, 2, 1, 3).reshape(-1, ndp * slice_ff)[:shard].astype(F32)

    gate_out, up_out = joined(0), joined(1)

    def shares(grad):
        return grad.astype(BF16).reshape(ndp, 2, -1, grad.shape[1])

    def reduce_chip(grad):
        mine = lax.dynamic_index_in_dim(grad, my_core, 1, False)
        theirs = lax.dynamic_index_in_dim(grad, 1 - my_core, 1, False)
        chip = (mine.astype(F32) + swap_core(theirs).astype(F32)).astype(BF16)
        return scatter_dp([lax.dynamic_index_in_dim(chip, my_dp ^ step, 0, False) for step in range(ndp)])

    carry = None
    back = []
    for chunk, state, d_resid in zip(chunks, kept, d_resids):
        absorbed, mixed, lse, heads_out, resid = state[:5]
        d_heads = after(mm_nt(d_resid.astype(BF16), out_w).astype(BF16), turn)
        out = attention_backward(
            *chunk, tables, table, latents, queries, key_w, value_w, absorbed, mixed, lse, d_heads, carry
        )
        if carry is None:
            d_queries, d_lat, carry, key_grad, value_grad = out
        else:
            d_queries, d_lat, key_grad, value_grad = out
        core_sum = d_lat[:nz].astype(F32) + swap_core(d_lat[nz:]).astype(F32)
        send = core_sum.astype(BF16)
        d_latent = core_sum[0]
        for step in range(1, nz):
            d_latent = d_latent + from_ahead(send[step], step).astype(F32)
        d_latent = d_latent.astype(BF16).reshape(-1, lat_width)
        back.append((d_queries, d_latent, heads_out, d_resid, resid, key_grad, value_grad))
        turn = send

    back = back[::-1]
    d_queries, d_latent, heads_out, d_resid, resid = (jnp.concatenate(parts) for parts in list(zip(*back))[:5])
    size = rows // 2
    d_queries = after(d_queries, ff_reduced)
    key_grad = back[0][5] + back[1][5]
    value_grad = back[0][6] + back[1][6]
    out_grad_w = reduce_chip(shares(mm_tn(heads_out, d_resid.astype(BF16))))
    d_normed = mm_nt(d_queries, query_w) + mm_nt(d_latent, latent_w)
    tokens_grad = (d_resid + norm_pull(tok, inv_one, gain_one, d_normed)).astype(BF16)
    size = chunks[0][1] * strip
    block = [
        jnp.concatenate(
            [
                out_part[ndp * size + i * (rows - size) : ndp * size + (i + 1) * (rows - size)],
                out_part[i * size : (i + 1) * size],
            ]
        )
        for i in range(ndp)
    ]
    layer_out = (resid + scatter_dp(block)).astype(BF16)

    grad_pack = jnp.concatenate(
        [
            shares(mm_tn(normed, d_queries)),
            shares(key_grad),
            shares(value_grad),
            shares(mm_tn(normed, d_latent)).reshape(ndp, 2, -1, width),
        ],
        axis=2,
    )
    grad_pack = jnp.concatenate([reduce_chip(grad_pack), out_grad_w]).astype(BF16)
    own = after(tiles(grad_pack), ff_pack)
    own = own.reshape(nz, -1, 8, 128)
    own = lax.psum_scatter(own, "z", scatter_dimension=0, tiled=True)
    own = lax.all_gather(own[0], SEQ, axis=0)
    own = own.reshape(nz, 2, -1, 8, 128).transpose(1, 0, 2, 3, 4).reshape(2, -1, 8, 128)
    grad_pack = untiled(own, *grad_pack.shape).astype(F32)
    lat_rows = half * lat_width // width
    cuts = [half, half + up_half, half + 2 * up_half, half + 2 * up_half + lat_rows]
    query_out, key_out, value_out, latent_out, out_out = (
        grad_pack[:, a:b].reshape(-1, width) for a, b in zip([0, *cuts], [*cuts, grad_pack.shape[1]])
    )
    latent_out = latent_out.reshape(shard, lat_width)

    def weighed(weight, grad):
        return jnp.sum(weight.astype(F32) * grad, axis=1)

    gain_one_out = (weighed(w_query, query_out) + weighed(w_latent, latent_out)) / norm1_gain.astype(F32)
    gain_two_out = (weighed(w_gate, gate_out) + weighed(w_up, up_out)) / norm2_gain.astype(F32)

    shape = (1, pieces, strip, width)
    return (
        layer_out.reshape(shape), tokens_grad.reshape(shape), gain_one_out, query_out, latent_out, key_out,
        value_out, out_out, gain_two_out, gate_out, up_out, down_out,
    )


def solution(mesh):
    sizes = mesh.shape
    grid = Mesh(mesh.devices.reshape(sizes["dp"], sizes["seq"] // 2, 2), ("dp", "z", "core"))
    stream = P("dp", None, SEQ, None)
    vector, matrix = P("dp"), P("dp", None)
    in_specs = (
        stream, vector, matrix, matrix, matrix, matrix, matrix, vector, matrix, matrix, matrix, stream, matrix,
    )
    out_specs = (
        stream, stream, vector, matrix, matrix, matrix, matrix, matrix, vector, matrix, matrix, matrix,
    )
    return jax.shard_map(per_device, mesh=grid, in_specs=in_specs, out_specs=out_specs, check_vma=False)
```

```python
import functools
import math

import jax
import jax.numpy as jnp
from jax import lax
from jax.experimental import pallas as pl
from jax.experimental.pallas import tpu as pltpu
from jax.sharding import Mesh
from jax.sharding import PartitionSpec as P

HEADS = 16
HEAD_DIM = 64
GROUPS = 2
LATENT = 256
PER_GROUP = HEADS // GROUPS
GROUP_COLS = PER_GROUP * HEAD_DIM
KEY_BLOCK = 256
VMEM_FORWARD = 56
VMEM_BACKWARD = 56
SCALE = 1.0 / math.sqrt(HEAD_DIM)
NEG_FILL = -1e30
NORM_EPS = 1e-05
F32 = jnp.float32
BF16 = jnp.bfloat16
DP = "dp"
SEQ = ("z", "core")
CHIP = ("dp", "core")


def mm(a, b):
    return jnp.dot(a, b, preferred_element_type=F32)


def mm_nt(a, b):
    return lax.dot_general(a, b, (((1,), (1,)), ((), ())), preferred_element_type=F32)


def mm_tn(a, b):
    return lax.dot_general(a, b, (((0,), (0,)), ((), ())), preferred_element_type=F32)


def low_lanes(rows):
    return lax.broadcasted_iota(jnp.int32, (rows, 2 * HEAD_DIM), 1) < HEAD_DIM


def pair_cols(pair):
    return slice(2 * HEAD_DIM * pair, 2 * HEAD_DIM * (pair + 1))


def expand_pair(part, proj):
    low = low_lanes(part.shape[0])
    zero = jnp.zeros_like(part)
    both = jnp.concatenate([jnp.where(low, part, zero), jnp.where(low, zero, part)], axis=0)
    return mm_nt(both, proj)


def shrink_pair(parts, proj):
    rows = parts.shape[0] // 2
    both = mm(parts, proj)
    return jnp.where(low_lanes(rows), both[:rows], both[rows:])


def outer_pair(parts, vals):
    rows = vals.shape[0]
    return jnp.where(low_lanes(LATENT), mm_tn(parts[:rows], vals), mm_tn(parts[rows:], vals))


def load_keys(lat_ref, slot_ref, block, strips, per_piece):
    piece = block // per_piece
    first = (block - piece * per_piece) * strips
    parts = [lat_ref[slot_ref[first + i], piece] for i in range(strips)]
    return jnp.concatenate(parts, axis=0), piece, first


def visible(block, base, starts, rows):
    key_pos = block * KEY_BLOCK + lax.broadcasted_iota(jnp.int32, (KEY_BLOCK, 2 * rows), 0)
    row_pos = base + lax.broadcasted_iota(jnp.int32, (KEY_BLOCK, 2 * rows), 1) % rows
    return (key_pos >= starts) & (key_pos <= row_pos)


def masked(scores, seen):
    wide = seen.shape[1]
    parts = [
        jnp.where(seen, scores[:, i * wide : (i + 1) * wide], NEG_FILL) for i in range(scores.shape[1] // wide)
    ]
    return jnp.concatenate(parts, axis=1)


def copies(sources, target_ref, sem):
    return [
        pltpu.make_async_copy(source, target_ref.at[slot], sem.at[slot]) for slot, source in enumerate(sources)
    ]


def latent_cols(group):
    return slice(group * LATENT, (group + 1) * LATENT)


def forward_body(first_piece, nseq, waits, lo_ref, hi_ref, base_ref, slot_ref, *refs):
    sources, refs = refs[:nseq], refs[nseq + waits :]
    start_ref, query_ref, key_up_ref, value_up_ref = refs[:4]
    abs_ref, mixed_ref, lse_ref, out_ref, top_ref, sum_ref, acc_ref, lat_ref, lat_sem = refs[4:]
    fetches = copies(sources, lat_ref, lat_sem)
    for fetch in fetches:
        fetch.start()
    strip = lat_ref.shape[2]
    groups, _, count = mixed_ref.shape[:3]
    strips = KEY_BLOCK // strip
    per_piece = nseq // strips
    tall = PER_GROUP * strip
    pairs = PER_GROUP // 2
    for pair in range(groups * pairs):
        cols = pair_cols(pair)
        part = expand_pair(query_ref[:, cols], key_up_ref[:, cols])
        part = part.astype(BF16) * jnp.asarray(SCALE, BF16)
        first = 2 * (pair % pairs)
        abs_ref[pair // pairs, first : first + 2] = part.reshape(2, count, strip, LATENT)
    for fetch in fetches:
        fetch.wait()

    for index in range(count):
        piece_id = index + first_piece
        top_ref[...] = jnp.full(top_ref.shape, NEG_FILL, F32)
        sum_ref[...] = jnp.zeros(sum_ref.shape, F32)
        acc_ref[...] = jnp.zeros(acc_ref.shape, F32)
        starts = jnp.broadcast_to(start_ref[index, 0:1], (KEY_BLOCK, 2 * strip))

        def step(block, carry):
            keys, _, _ = load_keys(lat_ref, slot_ref, block, strips, per_piece)
            keys = [keys[:, latent_cols(g)] for g in range(groups)]
            seen = visible(block, base_ref[piece_id], starts, strip)
            tops = [top_ref[g] for g in range(groups)]
            sums = [sum_ref[g] for g in range(groups)]
            raw = [mm_nt(keys[g], abs_ref[g, :, index].reshape(tall, LATENT)) for g in range(groups)]
            done = []
            for g in range(groups):
                scores = masked(raw[g], seen)
                new_top = jnp.maximum(tops[g], jnp.max(scores, axis=0, keepdims=True))
                shrink = jnp.exp(tops[g] - new_top)
                probs = jnp.exp(scores - new_top)
                total = sums[g] * shrink + jnp.sum(probs, axis=0, keepdims=True)
                done.append((new_top, total, shrink, mm_tn(keys[g], probs.astype(BF16))))
            for g in range(groups):
                new_top, total, shrink, term = done[g]
                top_ref[g] = new_top
                sum_ref[g] = total
                acc_ref[g] = acc_ref[g] * shrink + term
            return carry

        lax.fori_loop(lo_ref[piece_id], hi_ref[piece_id], step, 0)
        for g in range(groups):
            total = sum_ref[g]
            lse_ref[g, index] = jnp.broadcast_to(top_ref[g] + jnp.log(total), (8, tall))
            mixed = (acc_ref[g] * (1.0 / total)).T.astype(BF16)
            mixed_ref[g, :, index] = mixed.reshape(PER_GROUP, strip, LATENT)

    for pair in range(groups * pairs):
        cols = pair_cols(pair)
        first = 2 * (pair % pairs)
        parts = mixed_ref[pair // pairs, first : first + 2].reshape(2 * count * strip, LATENT)
        out_ref[:, cols] = shrink_pair(parts, value_up_ref[:, cols]).astype(BF16)


def backward_body(nseq, waits, lo_ref, hi_ref, base_ref, slot_ref, place_ref, *refs):
    sources, refs = refs[:nseq], refs[nseq + waits :]
    start_ref, query_ref, key_up_ref, value_up_ref, normed_ref, out_ref, resid_grad_ref, normed_hbm = refs[:8]
    abs_front, abs_back, mixed_front, mixed_back, lse_front, lse_back, grad_ref = refs[8:15]
    dquery_ref, dlat_hbm, mine_ref, theirs_ref = refs[15:19]
    dmix_ref, delta_ref, acc_ref, dabs_ref, dkey_ref, latent_sum_ref, stage_ref, lat_ref, lat_sem = refs[19:28]
    stream_ref, stream_sem, dlat_sem = refs[28:]
    fetches = copies(sources, lat_ref, lat_sem)
    for fetch in fetches:
        fetch.start()
    _, pieces, strip, _ = lat_ref.shape
    groups, _, cut = mixed_front.shape[:3]
    strips = KEY_BLOCK // strip
    per_piece = nseq // strips
    tall = PER_GROUP * strip
    pairs = PER_GROUP // 2
    depth = stream_ref.shape[0]
    my_core, my_dp = place_ref[0], place_ref[1]
    ndp = mine_ref.shape[0]

    def fetch_stream(seq):
        slot = seq % depth
        return pltpu.make_async_copy(normed_hbm.at[seq], stream_ref.at[slot], stream_sem.at[slot])

    for seq in range(depth):
        fetch_stream(seq).start()

    def give(first, grad):
        rows = grad.shape[0] // (2 * ndp)
        for dp in range(ndp):
            for core in range(2):
                part = grad[(2 * dp + core) * rows : (2 * dp + core + 1) * rows]

                @pl.when(my_core == core)
                def _():
                    mine_ref[dp ^ my_dp, first : first + rows] = part

                @pl.when(my_core != core)
                def _():
                    theirs_ref[dp ^ my_dp, first : first + rows] = part

    def of_pair(g, first):
        parts = [ref[g, first : first + 2] for ref in (mixed_front, mixed_back)]
        return jnp.concatenate(parts, axis=1).reshape(2 * pieces * strip, LATENT)

    def clear(slot, carry):
        dkey_ref[slot] = jnp.zeros(dkey_ref.shape[1:], F32)
        return carry

    lax.fori_loop(0, nseq, clear, 0)
    for pair in range(groups * pairs):
        cols = pair_cols(pair)
        g, first = pair // pairs, 2 * (pair % pairs)
        grads = grad_ref[:, cols]
        part = expand_pair(grads, value_up_ref[:, cols]).astype(BF16)
        dmix_ref[g, first : first + 2] = part.reshape(2, pieces, strip, LATENT)
        stage_ref[0, :, cols] = outer_pair(of_pair(g, first), grads).astype(BF16)
    for fetch in fetches:
        fetch.wait()

    for piece_id in range(pieces):
        index = piece_id if piece_id < cut else piece_id - cut
        front = piece_id < cut
        abs_ref, mixed_ref, lse_ref = (
            (abs_front, mixed_front, lse_front) if front else (abs_back, mixed_back, lse_back)
        )
        for g in range(groups):
            dmix_all = dmix_ref[g, :, piece_id].reshape(tall, LATENT).astype(F32)
            mixed_all = mixed_ref[g, :, index].reshape(tall, LATENT).astype(F32)
            delta = jnp.sum(dmix_all * mixed_all, axis=1, keepdims=True)
            delta_ref[g] = jnp.broadcast_to(delta, (tall, 128)).T[:8]
        acc_ref[...] = jnp.zeros(acc_ref.shape, F32)
        starts = jnp.broadcast_to(start_ref[piece_id, 0:1], (KEY_BLOCK, 2 * strip))

        def step(block, carry):
            keys, key_piece, first = load_keys(lat_ref, slot_ref, block, strips, per_piece)
            keys = [keys[:, latent_cols(g)] for g in range(groups)]
            seen = visible(block, base_ref[piece_id], starts, strip)
            absorbed = [abs_ref[g, :, index].reshape(tall, LATENT) for g in range(groups)]
            dmix = [dmix_ref[g, :, piece_id].reshape(tall, LATENT) for g in range(groups)]
            raw = [(mm_nt(keys[g], absorbed[g]), mm_nt(keys[g], dmix[g])) for g in range(groups)]
            done = []
            for g in range(groups):
                probs = jnp.exp(masked(raw[g][0] - lse_ref[g, index, 0:1], seen))
                d_scores = (probs * (raw[g][1] - delta_ref[g, 0:1])).astype(BF16)
                d_keys = mm(d_scores, absorbed[g]) + mm(probs.astype(BF16), dmix[g])
                done.append((mm_tn(d_scores, keys[g]), d_keys))
            for g in range(groups):
                acc_ref[g] += done[g][0]
                for i in range(strips):
                    part = done[g][1][i * strip : (i + 1) * strip]
                    dkey_ref[slot_ref[first + i], key_piece, :, latent_cols(g)] += part
            return carry

        lax.fori_loop(lo_ref[piece_id], hi_ref[piece_id], step, 0)
        for g in range(groups):
            dabs_ref[g, :, piece_id] = (acc_ref[g] * SCALE).astype(BF16).reshape(PER_GROUP, strip, LATENT)

    def settle(slot, carry):
        lat_ref[slot] = dkey_ref[slot].astype(BF16)
        return carry

    lax.fori_loop(0, nseq, settle, 0)
    send = pltpu.make_async_copy(lat_ref, dlat_hbm, dlat_sem)
    send.start()
    for pair in range(groups * pairs):
        cols = pair_cols(pair)
        g, first = pair // pairs, 2 * (pair % pairs)
        parts = dabs_ref[g, first : first + 2].reshape(2 * pieces * strip, LATENT)
        dquery_ref[:, cols] = shrink_pair(parts, key_up_ref[:, cols]).astype(BF16)
        stage_ref[1, :, cols] = outer_pair(parts, query_ref[:, cols]).astype(BF16)

    width = normed_ref.shape[1]
    half = width // (2 * ndp)
    up_half = LATENT // (2 * ndp)
    give(0, mm_tn(normed_ref[...], dquery_ref[...]).astype(BF16))
    give(half, stage_ref[1])
    give(half + up_half, stage_ref[0])
    give(half + 2 * up_half, mm_tn(out_ref[...], resid_grad_ref[...]).astype(BF16))
    latent_sum_ref[...] = jnp.zeros(latent_sum_ref.shape, F32)

    def latent_term(seq, carry):
        fetch_stream(seq).wait()
        rows = stream_ref[seq % depth].reshape(pieces * strip, width)
        grads = lat_ref[slot_ref[seq]].reshape(pieces * strip, groups * LATENT)
        latent_sum_ref[...] += mm_tn(rows, grads)

        @pl.when(seq + depth < nseq)
        def _():
            fetch_stream(seq + depth).start()

        return carry

    lax.fori_loop(0, nseq, latent_term, 0)
    lat_width = groups * LATENT
    fold = width // lat_width
    latent_grad = latent_sum_ref[...].astype(BF16).reshape(2 * ndp, fold, half // fold, lat_width)
    latent_grad = [latent_grad[:, i].reshape(width // fold, lat_width) for i in range(fold)]
    give(2 * half + 2 * up_half, jnp.concatenate(latent_grad, axis=1))
    send.wait()


def attention_specs(strip, pieces):
    tall = PER_GROUP * strip

    def whole(*shape):
        return pl.BlockSpec(shape, lambda *_: (0,) * len(shape), pipeline_mode=pl.Buffered(1))

    table = whole(pieces, 8, 2 * strip)
    rows = whole(pieces * strip, GROUPS * GROUP_COLS)
    proj = whole(LATENT, GROUPS * GROUP_COLS)
    heads = whole(GROUPS, PER_GROUP, pieces, strip, LATENT)
    lse = whole(GROUPS, pieces, 8, tall)
    return whole, table, rows, proj, heads, lse


def kernel_params(vmem):
    return pltpu.CompilerParams(dimension_semantics=("arbitrary",), vmem_limit_bytes=vmem << 20)


def attention_cost(nseq, pieces, strip, matmuls):
    pairs = HEADS * pieces * strip * nseq * strip * 2
    return pl.CostEstimate(
        flops=2 * matmuls * pairs * LATENT, transcendentals=pairs, bytes_accessed=32 << 20
    )


def attention_forward(first_piece, pieces, tables, table, latents, queries, key_up, value_up, waits):
    nseq = len(latents)
    strip = latents[0].shape[1]
    tall = PER_GROUP * strip
    _, t_spec, row_spec, proj_spec, head_spec, lse_spec = attention_specs(strip, pieces)
    head_shape = jax.ShapeDtypeStruct((GROUPS, PER_GROUP, pieces, strip, LATENT), BF16)
    in_place = pl.BlockSpec(memory_space=pl.ANY)
    return pl.pallas_call(
        functools.partial(forward_body, first_piece, nseq, len(waits)),
        name="attention_forward",
        grid_spec=pltpu.PrefetchScalarGridSpec(
            num_scalar_prefetch=len(tables),
            grid=(1,),
            in_specs=[in_place] * (nseq + len(waits)) + [t_spec, row_spec, proj_spec, proj_spec],
            out_specs=[head_spec, head_spec, lse_spec, row_spec],
            scratch_shapes=[
                pltpu.VMEM((GROUPS, 1, tall), F32),
                pltpu.VMEM((GROUPS, 1, tall), F32),
                pltpu.VMEM((GROUPS, LATENT, tall), F32),
                pltpu.VMEM((nseq, *latents[0].shape), BF16),
                pltpu.SemaphoreType.DMA((nseq,)),
            ],
        ),
        out_shape=[
            head_shape,
            head_shape,
            jax.ShapeDtypeStruct((GROUPS, pieces, 8, tall), F32),
            jax.ShapeDtypeStruct((pieces * strip, queries.shape[1]), BF16),
        ],
        compiler_params=kernel_params(VMEM_FORWARD if nseq <= 8 else 56),
        cost_estimate=attention_cost(nseq, pieces, strip, 2),
    )(*tables, *latents, *waits, table, queries, key_up, value_up)


def attention_backward(
    tables, place, latents, table, queries, key_up, value_up, normed, heads_out, resid_grads, normed_stream,
    absorbed, mixed, lse, grads, ndp, waits,
):
    nseq = len(latents)
    pieces, strip, lat_width = latents[0].shape
    tall = PER_GROUP * strip
    cut = mixed[0].shape[2]
    whole, t_spec, row_spec, proj_spec, _, _ = attention_specs(strip, pieces)
    head_front, lse_front = attention_specs(strip, cut)[4:]
    head_back, lse_back = attention_specs(strip, pieces - cut)[4:]
    width = normed_stream.shape[3]
    depth = nseq if nseq <= 8 else 2
    part = (ndp, (2 * width + 2 * LATENT + lat_width * width // key_up.shape[1]) // (2 * ndp), width)
    in_place = pl.BlockSpec(memory_space=pl.ANY)
    return pl.pallas_call(
        functools.partial(backward_body, nseq, len(waits)),
        name="attention_backward",
        grid_spec=pltpu.PrefetchScalarGridSpec(
            num_scalar_prefetch=len(tables) + 1,
            grid=(1,),
            in_specs=[in_place] * (nseq + len(waits)) + [
                t_spec, row_spec, proj_spec, proj_spec, row_spec, row_spec, row_spec, in_place,
                head_front, head_back, head_front, head_back, lse_front, lse_back, row_spec,
            ],
            out_specs=[row_spec, in_place, whole(*part), whole(*part)],
            scratch_shapes=[
                pltpu.VMEM((GROUPS, PER_GROUP, pieces, strip, LATENT), BF16),
                pltpu.VMEM((GROUPS, 8, tall), F32),
                pltpu.VMEM((GROUPS, tall, LATENT), F32),
                pltpu.VMEM((GROUPS, PER_GROUP, pieces, strip, LATENT), BF16),
                pltpu.VMEM((nseq, pieces, strip, lat_width), F32),
                pltpu.VMEM((width, lat_width), F32),
                pltpu.VMEM((2, LATENT, GROUPS * GROUP_COLS), BF16),
                pltpu.VMEM((nseq, pieces, strip, lat_width), BF16),
                pltpu.SemaphoreType.DMA((nseq,)),
                pltpu.VMEM((depth, *normed_stream.shape[1:]), BF16),
                pltpu.SemaphoreType.DMA((depth,)),
                pltpu.SemaphoreType.DMA,
            ],
        ),
        out_shape=[
            jax.ShapeDtypeStruct(queries.shape, BF16),
            jax.ShapeDtypeStruct((nseq, pieces, strip, lat_width), BF16),
            jax.ShapeDtypeStruct(part, BF16),
            jax.ShapeDtypeStruct(part, BF16),
        ],
        compiler_params=kernel_params(VMEM_BACKWARD if nseq <= 8 else 62),
        cost_estimate=attention_cost(nseq, pieces, strip, 5),
    )(
        *tables, place, *latents, *waits, table, queries, key_up, value_up, normed, heads_out, resid_grads, normed_stream,
        *absorbed, *mixed, *lse, grads,
    )


def positions_body(pieces, nz, strip, place_ref, lengths_ref, table_ref, lo_ref, hi_ref, base_ref, slot_ref):
    my_core, my_z = place_ref[0], place_ref[2]
    span = strip * 2 * nz
    mine = (2 * my_z + my_core) * strip
    wide = table_ref.shape[2]
    lane = lax.broadcasted_iota(jnp.int32, (1, wide), 1) % strip
    positions = [piece * span + mine + lane for piece in range(pieces)]
    ids = [piece * span + mine for piece in range(pieces)]

    def entry(i, carry):
        first, starts, lows = carry
        end = first + lengths_ref[0, 2 * i]
        starts = [jnp.where((p >= first) & (p < end), first, s) for p, s in zip(positions, starts)]
        lows = [jnp.where((p >= first) & (p < end), first, s) for p, s in zip(ids, lows)]
        return end + lengths_ref[0, 2 * i + 1], starts, lows

    _, starts, lows = lax.fori_loop(0, lengths_ref.shape[1] // 2, entry, (jnp.int32(0), positions, ids))
    for piece in range(pieces):
        table_ref[piece] = jnp.broadcast_to(starts[piece], table_ref.shape[1:])
        lo_ref[piece] = lows[piece] // KEY_BLOCK
        hi_ref[piece] = (ids[piece] + strip + KEY_BLOCK - 1) // KEY_BLOCK
        base_ref[piece] = ids[piece]
    for seq in range(2 * nz):
        core = jnp.where(my_core == seq % 2, 0, 1)
        slot_ref[seq] = core * nz + jnp.where(my_z >= seq // 2, my_z - seq // 2, my_z - seq // 2 + nz)


def positions_of(place, lengths, pieces, nz, strip):
    small = pl.BlockSpec(memory_space=pltpu.SMEM)
    counts = [pieces, pieces, pieces, 2 * nz]
    table, *tables = pl.pallas_call(
        functools.partial(positions_body, pieces, nz, strip),
        name="positions",
        grid_spec=pltpu.PrefetchScalarGridSpec(
            num_scalar_prefetch=1,
            grid=(1,),
            in_specs=[small],
            out_specs=[whole_spec(pieces, 8, 2 * strip)] + [small] * 4,
        ),
        out_shape=[jax.ShapeDtypeStruct((pieces, 8, 2 * strip), jnp.int32)]
        + [jax.ShapeDtypeStruct((count,), jnp.int32) for count in counts],
        cost_estimate=pl.CostEstimate(flops=4096, transcendentals=0, bytes_accessed=16384),
    )(place, lengths)
    return table, tuple(tables)


def cut_body(place_ref, gate_hbm, up_hbm, out_ref, rows_ref, sems):
    ndp, _, half, wide = out_ref.shape
    first = pl.multiple_of(place_ref[0] * half, half)
    fetches = [
        pltpu.make_async_copy(source.at[pl.ds(first, half)], rows_ref.at[i], sems.at[i])
        for i, source in enumerate((gate_hbm, up_hbm))
    ]
    for fetch in fetches:
        fetch.start()
    slice_ff = gate_hbm.shape[1] // ndp
    low = lax.broadcasted_iota(jnp.int32, (half, 128), 1) < 64
    zero = jnp.zeros((half, 128), F32)
    whole_tiles = slice_ff // 128
    for which, fetch in enumerate(fetches):
        fetch.wait()

        def tile_of(t):
            return rows_ref[which, :, t * 128 : (t + 1) * 128].astype(F32)

        for dp in range(ndp):
            first_tile = dp * slice_ff // 128
            if dp % 2 == 0:
                parts = [tile_of(first_tile + t) for t in range(whole_tiles)]
                parts.append(jnp.where(low, tile_of(first_tile + whole_tiles), zero))
            else:
                halves = [pltpu.roll(tile_of(first_tile + t), 64, 1) for t in range(whole_tiles + 1)]
                parts = [jnp.where(low, halves[t], halves[t + 1]) for t in range(whole_tiles)]
                parts.append(jnp.where(low, halves[whole_tiles], zero))
            for t, part in enumerate(parts):
                out_ref[dp, which, :, t * 128 : (t + 1) * 128] = part.astype(BF16)


def cut_columns(place, w_gate, w_up, ndp, half):
    ff = w_gate.shape[1]
    wide = -(-ff // ndp // 128) * 128
    in_place = pl.BlockSpec(memory_space=pl.ANY)
    return pl.pallas_call(
        cut_body,
        name="cut_columns",
        grid_spec=pltpu.PrefetchScalarGridSpec(
            num_scalar_prefetch=1,
            grid=(1,),
            in_specs=[in_place, in_place],
            out_specs=whole_spec(ndp, 2, half, wide),
            scratch_shapes=[pltpu.VMEM((2, half, ff), BF16), pltpu.SemaphoreType.DMA((2,))],
        ),
        out_shape=jax.ShapeDtypeStruct((ndp, 2, half, wide), BF16),
        compiler_params=kernel_params(16),
        cost_estimate=pl.CostEstimate(flops=half * ff, transcendentals=0, bytes_accessed=3 << 20),
    )(place, w_gate, w_up)


def front_body(ndp, place_ref, tok_ref, *refs):
    blocks, refs = refs[:ndp], refs[ndp:]
    other_hbm, normed_ref, latent_ref, gain_out_ref, weight_ref, gain_ref, sems = refs
    my_core, my_dp = place_ref[0], place_ref[1]
    half = other_hbm.shape[1] - 16
    width = tok_ref.shape[1]
    shard = 2 * half
    fetches = []
    for i in range(ndp):
        dp = my_dp ^ i
        for core, source in enumerate((blocks[i], other_hbm.at[i])):
            first = pl.multiple_of(dp * shard + (my_core ^ core) * half, half)
            fetches.append((source.at[pl.ds(0, half)], weight_ref.at[pl.ds(first, half)]))
        fetches.append((blocks[i].at[pl.ds(half, 16)], gain_ref.at[dp]))
    fetches = [pltpu.make_async_copy(a, b, sems.at[i]) for i, (a, b) in enumerate(fetches)]
    for fetch in fetches:
        fetch.start()
    tok = tok_ref[...].astype(F32)
    scaled = tok * inverse_rms(tok)
    for fetch in fetches:
        fetch.wait()
    gains = [gain_ref[dp].astype(F32) for dp in range(ndp)]
    gain_one = jnp.concatenate([g[0:1, :shard] for g in gains], axis=1)
    gain_two = jnp.concatenate([g[0:1, shard : 2 * shard] for g in gains], axis=1)
    normed = (scaled * gain_one).astype(BF16)
    normed_ref[...] = normed
    latent_ref[...] = mm(normed, weight_ref[...]).astype(BF16)
    gain_out_ref[0:8] = jnp.broadcast_to(gain_one, (8, width))
    gain_out_ref[8:16] = jnp.broadcast_to(gain_two, (8, width))


def front(place, tok, blocks, other):
    rows, width = tok.shape
    ndp = len(blocks)
    lat_width = other.shape[2]
    in_place = pl.BlockSpec(memory_space=pl.ANY)
    return pl.pallas_call(
        functools.partial(front_body, ndp),
        name="front",
        grid_spec=pltpu.PrefetchScalarGridSpec(
            num_scalar_prefetch=1,
            grid=(1,),
            in_specs=[whole_spec(rows, width)] + [in_place] * (ndp + 1),
            out_specs=[
                whole_spec(rows, width), whole_spec(rows, lat_width), whole_spec(16, width),
                whole_spec(width, lat_width),
            ],
            scratch_shapes=[
                pltpu.VMEM((ndp, 16, lat_width), BF16),
                pltpu.SemaphoreType.DMA((3 * ndp,)),
            ],
        ),
        out_shape=[
            jax.ShapeDtypeStruct((rows, width), BF16),
            jax.ShapeDtypeStruct((rows, lat_width), BF16),
            jax.ShapeDtypeStruct((16, width), F32),
            jax.ShapeDtypeStruct((width, lat_width), BF16),
        ],
        compiler_params=kernel_params(16),
        cost_estimate=pl.CostEstimate(
            flops=2 * rows * width * lat_width, transcendentals=rows, bytes_accessed=3 << 20
        ),
    )(place, tok, *blocks, other)


def ff_body(ndp, first_row, waits, place_ref, *refs):
    blocks, refs = refs[:ndp], refs[ndp + waits :]
    grad_hbm, mine_hbm, theirs_hbm, down_hbm = refs[:4]
    hidden_ref, dgate_ref, dup_ref = refs[4:7]
    part_refs, refs = refs[7 : 7 + ndp], refs[7 + ndp :]
    weight_ref, down_ref, grad_ref, weight_sem, down_sem, grad_sem = refs
    my_core, my_dp = place_ref[0], place_ref[1]
    size, width = blocks[0].shape
    slice_ff = down_hbm.shape[0]
    wide = hidden_ref.shape[1]
    half = mine_hbm.shape[2]
    fetch_down = pltpu.make_async_copy(down_hbm, down_ref.at[pl.ds(0, slice_ff)], down_sem)
    fetch_down.start()
    fetch_grads = [
        pltpu.make_async_copy(
            grad_hbm.at[my_dp ^ i, pl.ds(first_row, size)], grad_ref.at[pl.ds(i * size, size)], grad_sem.at[i]
        )
        for i in range(ndp)
    ]
    for fetch in fetch_grads:
        fetch.start()
    fetch_weights = []
    for which in range(2):
        for dp in range(ndp):
            for core, source in enumerate((mine_hbm, theirs_hbm)):
                first = pl.multiple_of((2 * dp + (my_core ^ core)) * half, half)
                fetch_weights.append(
                    pltpu.make_async_copy(
                        source.at[dp, which], weight_ref.at[which, pl.ds(first, half)],
                        weight_sem.at[which, 2 * dp + core],
                    )
                )
    for fetch in fetch_weights:
        fetch.start()
    if wide > slice_ff:
        down_ref[slice_ff:] = jnp.zeros((wide - slice_ff, width), BF16)
    fetch_down.wait()
    for fetch in fetch_grads + fetch_weights:
        fetch.wait()
    per = max(ndp // 2, 1)
    for first in range(0, ndp, per):
        span = slice(first * size, (first + per) * size)
        normed = jnp.concatenate([blocks[i][...] for i in range(first, first + per)], axis=0)
        gate = mm(normed, weight_ref[0])
        up = mm(normed, weight_ref[1])
        d_hidden = mm_nt(grad_ref[span], down_ref[...])
        sig = 1.0 / (1.0 + jnp.exp(-gate))
        silu = gate * sig
        hidden_ref[span] = (silu * up).astype(BF16)
        d_gate = (d_hidden * up * (sig * (1.0 + gate * (1.0 - sig)))).astype(BF16)
        d_up = (d_hidden * silu).astype(BF16)
        dgate_ref[span] = d_gate
        dup_ref[span] = d_up
        part = (mm_nt(d_gate, weight_ref[0]) + mm_nt(d_up, weight_ref[1])).astype(BF16)
        for i in range(per):
            part_refs[first + i][...] = part[i * size : (i + 1) * size]


def whole_spec(*shape):
    return pl.BlockSpec(shape, lambda *_: (0,) * len(shape), pipeline_mode=pl.Buffered(1))


def feed_forward(place, first_row, blocks, grad_blocks, mine, theirs, down, waits):
    ndp = len(blocks)
    size, width = blocks[0].shape
    wide = mine.shape[3]
    in_place = pl.BlockSpec(memory_space=pl.ANY)
    tall = jax.ShapeDtypeStruct((ndp * size, wide), BF16)
    return pl.pallas_call(
        functools.partial(ff_body, ndp, first_row, len(waits)),
        name="feed_forward",
        grid_spec=pltpu.PrefetchScalarGridSpec(
            num_scalar_prefetch=1,
            grid=(1,),
            in_specs=[whole_spec(size, width)] * ndp + [in_place] * (len(waits) + 4),
            out_specs=[whole_spec(ndp * size, wide)] * 3 + [whole_spec(size, width)] * ndp,
            scratch_shapes=[
                pltpu.VMEM((2, width, wide), BF16),
                pltpu.VMEM((wide, width), BF16),
                pltpu.VMEM((ndp * size, width), BF16),
                pltpu.SemaphoreType.DMA((2, 2 * ndp)),
                pltpu.SemaphoreType.DMA,
                pltpu.SemaphoreType.DMA((ndp,)),
            ],
        ),
        out_shape=[tall] * 3 + [jax.ShapeDtypeStruct((size, width), BF16)] * ndp,
        compiler_params=kernel_params(48),
        cost_estimate=pl.CostEstimate(
            flops=10 * ndp * size * width * wide, transcendentals=ndp * size * wide, bytes_accessed=12 << 20
        ),
    )(place, *blocks, *waits, grad_blocks, mine, theirs, down)


def ff_grad_body(ndp, nseq, spans, owned, waits, place_ref, *refs):
    blocks, refs = refs[: ndp * len(spans)], refs[ndp * len(spans) + waits :]
    sides, refs = refs[: 3 * len(spans)], refs[3 * len(spans) :]
    grad_hbm, pack_ref, normed_ref, grad_ref, hidden_ref, dgate_ref, dup_ref, sems = refs
    my_dp = place_ref[1]
    width = normed_ref.shape[1]
    wide = hidden_ref.shape[1]
    down_rows, own_rows = owned
    fetches = []

    def fetch(source, target):
        copy = pltpu.make_async_copy(source, target, sems.at[len(fetches)])
        copy.start()
        fetches.append(copy)

    row = 0
    for chunk, (first_row, size) in enumerate(spans):
        for target, source in zip((hidden_ref, dgate_ref, dup_ref), sides[3 * chunk : 3 * chunk + 3]):
            fetch(source, target.at[pl.ds(row, ndp * size)])
        for i in range(ndp):
            fetch(blocks[ndp * chunk + i], normed_ref.at[pl.ds(row + i * size, size)])
            fetch(grad_hbm.at[my_dp ^ i, pl.ds(first_row, size)], grad_ref.at[pl.ds(row + i * size, size)])
        row += ndp * size
    for copy in fetches:
        copy.wait()

    def give(seq, first, part):
        rows = part.shape[0]
        for tile in range(part.shape[1] // 128):
            pack_ref[seq, first + tile * rows : first + (tile + 1) * rows] = part[:, tile * 128 : (tile + 1) * 128]

    some = wide // 2
    for first in range(0, wide, some):
        part = mm_tn(hidden_ref[:, first : first + some], grad_ref[...]).astype(BF16)
        for i in range(some // down_rows):
            give(first // down_rows + i, 0, part[i * down_rows : (i + 1) * down_rows])
    for seq in range(wide // down_rows, nseq):
        give(seq, 0, jnp.zeros((down_rows, width), BF16))
    shard = width // ndp
    first = down_rows * width // 128
    for dp in range(ndp):
        for side in (dgate_ref, dup_ref):
            part = mm_tn(normed_ref[:, dp * shard : (dp + 1) * shard], side[...]).astype(BF16)
            for seq in range(nseq):
                if seq * own_rows < shard:
                    give(seq, first, part[seq * own_rows : (seq + 1) * own_rows])
                else:
                    give(seq, first, jnp.zeros((own_rows, wide), BF16))
            first += own_rows * wide // 128


def ff_gradients(place, spans, blocks, sides, grad_blocks, nseq, owned, waits):
    ndp = len(blocks) // len(spans)
    width = blocks[0].shape[1]
    wide = sides[0].shape[1]
    rows = ndp * sum(size for _, size in spans)
    down_rows, own_rows = owned
    pack = (nseq, (down_rows * width + 2 * ndp * own_rows * wide) // 128, 128)
    in_place = pl.BlockSpec(memory_space=pl.ANY)
    count = len(spans) * (3 + 2 * ndp)
    return pl.pallas_call(
        functools.partial(ff_grad_body, ndp, nseq, spans, owned, len(waits)),
        name="feed_forward_gradients",
        grid_spec=pltpu.PrefetchScalarGridSpec(
            num_scalar_prefetch=1,
            grid=(1,),
            in_specs=[in_place] * (len(blocks) + len(waits) + len(sides) + 1),
            out_specs=whole_spec(*pack),
            scratch_shapes=[
                pltpu.VMEM((rows, width), BF16),
                pltpu.VMEM((rows, width), BF16),
                pltpu.VMEM((rows, wide), BF16),
                pltpu.VMEM((rows, wide), BF16),
                pltpu.VMEM((rows, wide), BF16),
                pltpu.SemaphoreType.DMA((count,)),
            ],
        ),
        out_shape=jax.ShapeDtypeStruct(pack, BF16),
        compiler_params=kernel_params(48),
        cost_estimate=pl.CostEstimate(
            flops=6 * rows * width * wide, transcendentals=0, bytes_accessed=16 << 20
        ),
    )(place, *blocks, *waits, *sides, grad_blocks)


def unpack_ff_body(ndp, own_rows, down_rows, pack_ref, gate_w_ref, up_w_ref, down_ref, gate_ref, up_ref, gain_ref):
    nseq = pack_ref.shape[0]
    slice_ff, width = down_ref.shape
    wide = -(-slice_ff // 128) * 128
    low = lax.broadcasted_iota(jnp.int32, (own_rows, 128), 1) < 64
    for seq in range(nseq):
        keep = min(down_rows, slice_ff - seq * down_rows)
        for tile in range(width // 128):
            if keep > 0:
                part = pack_ref[seq, tile * down_rows : (tile + 1) * down_rows].astype(F32)
                down_ref[seq * down_rows : seq * down_rows + keep, tile * 128 : (tile + 1) * 128] = part[:keep]
    for seq in range(gate_ref.shape[0] // own_rows):
        span = slice(seq * own_rows, (seq + 1) * own_rows)
        total = jnp.zeros((own_rows, 1), F32)
        for which, (out_ref, w_ref) in enumerate(((gate_ref, gate_w_ref), (up_ref, up_w_ref))):

            def tile_of(dp, tile):
                first = down_rows * width // 128 + ((2 * dp + which) * (wide // 128) + tile) * own_rows
                return pack_ref[seq, first : first + own_rows].astype(F32)

            whole_tiles = slice_ff // 128
            for dp in range(0, ndp, 2):
                first = dp * slice_ff // 128
                parts = [tile_of(dp, t) for t in range(whole_tiles)]
                halves = [pltpu.roll(tile_of(dp + 1, t), 64, 1) for t in range(whole_tiles + 1)]
                parts.append(jnp.where(low, tile_of(dp, whole_tiles), halves[0]))
                parts += [jnp.where(low, halves[t], halves[t + 1]) for t in range(whole_tiles)]
                for t, part in enumerate(parts):
                    cols = slice((first + t) * 128, (first + t + 1) * 128)
                    out_ref[span, cols] = part
                    total += jnp.sum(part * w_ref[span, cols].astype(F32), axis=1, keepdims=True)
        gain_ref[span] = jnp.broadcast_to(total, (own_rows, 128))


def unpack_ff(pack, w_gate, w_up, slice_ff, width, own_rows, down_rows):
    shard, ff = w_gate.shape
    full = jax.ShapeDtypeStruct((shard, ff), F32)
    return pl.pallas_call(
        functools.partial(unpack_ff_body, ff // slice_ff, own_rows, down_rows),
        name="unpack_feed_forward",
        grid=(1,),
        in_specs=[whole_spec(*pack.shape), whole_spec(shard, ff), whole_spec(shard, ff)],
        out_specs=[whole_spec(slice_ff, width), whole_spec(shard, ff), whole_spec(shard, ff), whole_spec(shard, 128)],
        out_shape=[
            jax.ShapeDtypeStruct((slice_ff, width), F32), full, full, jax.ShapeDtypeStruct((shard, 128), F32),
        ],
        compiler_params=kernel_params(40),
        cost_estimate=pl.CostEstimate(flops=4 * shard * ff, transcendentals=0, bytes_accessed=16 << 20),
    )(pack, w_gate, w_up)


def unpack_attention_body(
    sections, pack_ref, query_w_ref, latent_w_ref, query_ref, key_ref, value_ref, out_ref, latent_ref, gain_ref
):
    nz, _, rows, _ = pack_ref.shape
    step = 32
    for core in range(2):
        first = 0
        for section, target in zip(sections[:4], (query_ref, key_ref, value_ref, out_ref)):
            for row in range(0, section, step):
                place = first + row
                part = pack_ref[place // rows, core, place % rows : place % rows + step].astype(F32)
                target[core * section + row : core * section + row + step] = part
            first += section
        for row in range(0, sections[4], step):
            place = first + row
            part = pack_ref[place // rows, core, place % rows : place % rows + step].astype(F32)
            width = latent_ref.shape[1]
            for i in range(part.shape[1] // width):
                base = core * sections[0] + i * sections[4] + row
                latent_ref[base : base + step] = part[:, i * width : (i + 1) * width]
    total = jnp.sum(query_w_ref[...].astype(F32) * query_ref[...], axis=1, keepdims=True)
    total += jnp.sum(latent_w_ref[...].astype(F32) * latent_ref[...], axis=1, keepdims=True)
    gain_ref[...] = jnp.broadcast_to(total, gain_ref.shape)


def unpack_attention(pack, w_query, w_latent, sections):
    shard, width = w_query.shape
    lat_width = w_latent.shape[1]
    shapes = [
        (shard, width), (2 * sections[1], width), (2 * sections[2], width), (2 * sections[3], width),
        (shard, lat_width), (shard, 128),
    ]
    return pl.pallas_call(
        functools.partial(unpack_attention_body, sections),
        name="unpack_attention",
        grid=(1,),
        in_specs=[whole_spec(*pack.shape), whole_spec(shard, width), whole_spec(shard, lat_width)],
        out_specs=[whole_spec(*shape) for shape in shapes],
        out_shape=[jax.ShapeDtypeStruct(shape, F32) for shape in shapes],
        compiler_params=kernel_params(24),
        cost_estimate=pl.CostEstimate(flops=4 * shard * width, transcendentals=0, bytes_accessed=6 << 20),
    )(pack, w_query, w_latent)


def inverse_rms(values):
    return lax.rsqrt(jnp.mean(values * values, axis=-1, keepdims=True) + NORM_EPS)


def norm_pull(values, inverse, gain, grads):
    scaled = gain * grads
    return inverse * scaled - values * (inverse**3) * jnp.mean(scaled * values, axis=-1, keepdims=True)


def my_half(shard):
    half = shard.shape[0] // 2
    return lax.dynamic_slice_in_dim(shard, lax.axis_index("core") * half, half, 0)


def swap_core(x):
    return lax.ppermute(x, "core", [(0, 1), (1, 0)])


def partner(x, step):
    return lax.ppermute(x, DP, [(i, i ^ step) for i in range(lax.axis_size(DP))])


def from_behind(x, step):
    nz = lax.axis_size("z")
    return lax.ppermute(x, "z", [(i, (i + step) % nz) for i in range(nz)])


def from_ahead(x, step):
    nz = lax.axis_size("z")
    return lax.ppermute(x, "z", [((i + step) % nz, i) for i in range(nz)])


def gather_dp(x):
    return [x] + [partner(x, step) for step in range(1, lax.axis_size(DP))]


def scatter_dp(parts):
    total = parts[0].astype(F32)
    for step in range(1, len(parts)):
        total = total + partner(parts[step].astype(BF16), step).astype(F32)
    return total


def together(*arrays):
    return lax.optimization_barrier(arrays)


def per_device(
    tokens, norm1_gain, w_query, w_latent, w_key_up, w_value_up, w_out, norm2_gain,
    w_gate, w_up, w_down, out_grad, seq_lengths,
):
    ndp = lax.axis_size(DP)
    nz = lax.axis_size("z")
    nseq = 2 * nz
    pieces, strip, width = tokens.shape[1:]
    rows = pieces * strip
    lat_width = GROUPS * LATENT
    my_z, my_core, my_dp = lax.axis_index("z"), lax.axis_index("core"), lax.axis_index(DP)
    shard = norm1_gain.shape[0]
    slice_ff = w_down.shape[0]
    wide_ff = -(-slice_ff // 128) * 128
    half = shard // 2

    gains = jnp.pad(jnp.concatenate([norm1_gain, norm2_gain])[None, :], ((0, 15), (0, lat_width - 2 * shard)))
    own_head = jnp.concatenate([my_half(w_latent), gains], axis=0)
    place = jnp.stack([my_core, my_dp, my_z]).astype(jnp.int32)
    by_step = gather_dp(own_head)
    pack = lax.all_gather(
        jnp.concatenate([my_half(w_query), my_half(w_key_up), my_half(w_value_up), my_half(w_out)], axis=0),
        CHIP,
        axis=0,
    )

    table, tables = positions_of(place, seq_lengths, pieces, nz, strip)

    tok_rows = tokens[0].reshape(rows, width)
    normed, latent, gains, latent_w = front(place, tok_rows, by_step, swap_core(jnp.stack(by_step)))
    latent = latent.reshape(pieces, strip, lat_width)
    gain_one, gain_two = gains[0:1], gains[8:9]
    tok = tok_rows.astype(F32)
    inv_one = inverse_rms(tok)
    cut_ff, latent = together(cut_columns(place, w_gate, w_up, ndp, half), latent)
    sliced = lax.all_to_all(cut_ff, DP, 0, 0, tiled=True)
    behind = [from_behind(latent, step) for step in range(1, nz)]
    pack, *behind = together(pack, *behind)
    up_half = w_key_up.shape[0] // 2
    cuts = [0, half, half + up_half, half + 2 * up_half, 2 * half + 2 * up_half]
    pack, grad_in = together(pack, out_grad[0].reshape(rows, width))
    query_w, key_w, value_w, out_w = (pack[:, a:b].reshape(-1, width) for a, b in zip(cuts[:-1], cuts[1:]))
    queries = mm(normed, query_w).astype(BF16)
    core_lat = [latent, *behind]
    latents = core_lat + [swap_core(x) for x in core_lat]

    grad_rows = out_grad[0].reshape(rows, width)
    grad_blocks = lax.all_gather(grad_in, DP, axis=0)
    cut = pieces // 2
    chunks = [(cut, pieces - cut), (0, cut)]

    def rows_of(x, chunk):
        return x[chunk[0] * strip : (chunk[0] + chunk[1]) * strip]

    def pieces_of(x, chunk):
        return x[chunk[0] : chunk[0] + chunk[1]]

    kept = []
    for chunk in chunks:
        absorbed, mixed, lse, heads_out = attention_forward(
            *chunk, tables, pieces_of(table, chunk), latents, rows_of(queries, chunk), key_w, value_w,
            [kept[0][6][0], sliced] if kept else [],
        )
        if kept:
            heads_out, *fresh = together(heads_out, *kept[0][6])
            kept[0][6][:] = fresh
        resid = rows_of(tok, chunk) + mm(heads_out, out_w)
        inv_two = inverse_rms(resid)
        normed_two = (resid * inv_two * gain_two).astype(BF16)
        kept.append((absorbed, mixed, lse, heads_out, resid, inv_two, gather_dp(normed_two)))

    normed_in, kept[1][6][0] = together(normed, kept[1][6][0])
    normed_stream = lax.all_gather(normed_in.reshape(pieces, strip, width), SEQ, axis=0)

    sliced_other = swap_core(sliced)
    ff_sides = []
    ff_parts = []
    for chunk, state in zip(chunks, kept):
        blocks = state[6]
        out = feed_forward(
            place, chunk[0] * strip, blocks, grad_blocks, sliced, sliced_other, w_down,
            [ff_parts[0][0]] if ff_parts else [kept[1][6][0]],
        )
        ff_sides.append((blocks, out[:3]))
        ff_parts.append(out[3:])
    received = [[partner(x, step) for step, x in enumerate(parts) if step] for parts in ff_parts]
    d_resids = []
    for chunk, state, parts, others in zip(chunks, kept, ff_parts, received):
        resid, inv_two = state[4:6]
        d_normed_two = sum((x.astype(F32) for x in others), parts[0].astype(F32))
        d_resids.append(
            rows_of(grad_rows, chunk).astype(F32) + norm_pull(resid, inv_two, gain_two, d_normed_two)
        )

    down_rows = -(-slice_ff // (16 * nseq)) * 16
    own_rows = -(-shard // (16 * nseq)) * 16
    ff_pack = ff_gradients(
        place,
        [(chunk[0] * strip, chunk[1] * strip) for chunk in chunks],
        [x for blocks, _ in ff_sides for x in blocks],
        [x for _, sides in ff_sides for x in sides],
        grad_blocks,
        nseq,
        (down_rows, own_rows),
        [],
    )
    down_wide = jnp.pad(w_down, ((0, wide_ff - slice_ff), (0, 0)))
    ff_whole = ff_pack

    ff_pack = lax.psum_scatter(ff_pack, SEQ, scatter_dimension=0, tiled=True)[0]

    order_of = [chunks.index((0, cut)), chunks.index((cut, pieces - cut))]
    d_resid = jnp.concatenate([d_resids[i] for i in order_of])
    resid = jnp.concatenate([kept[i][4] for i in order_of])
    heads_out = jnp.concatenate([kept[i][3] for i in order_of])
    d_resid_round = d_resid.astype(BF16)
    d_heads = mm_nt(d_resid_round, out_w).astype(BF16)
    absorbed, mixed, lse = ([kept[i][which] for i in order_of] for which in range(3))
    d_queries, d_lat, part_mine, part_theirs = attention_backward(
        tables, place, latents, table, queries, key_w, value_w, normed, heads_out, d_resid_round, normed_stream,
        absorbed, mixed, lse, d_heads, ndp, [ff_whole],
    )
    ff_pack, part_theirs = together(ff_pack, part_theirs)
    part_other = swap_core(part_theirs)
    chip_parts = [
        (part_mine[i].astype(F32) + part_other[i].astype(F32)).astype(BF16) for i in range(ndp)
    ]
    d_lat, *chip_parts = together(d_lat, *chip_parts)
    out_sides = together(chip_parts[0], *[sides[0] for _, sides in ff_sides])
    chip_parts[0] = out_sides[0]
    out_parts = [mm(x, down_wide).astype(BF16) for x in out_sides[1:]]
    core_sum = d_lat[:nz].astype(F32) + swap_core(d_lat[nz:]).astype(F32)
    send = core_sum.astype(BF16)
    d_latent = core_sum[0]
    for step in range(1, nz):
        d_latent = d_latent + from_ahead(send[step], step).astype(F32)
    d_latent = d_latent.astype(BF16).reshape(rows, lat_width)
    down_lines = down_rows * width // 128
    swap = ff_pack[down_lines:].reshape(ndp, -1, 128)
    swap = lax.all_to_all(swap, DP, 0, 0, tiled=True)
    ff_pack = jnp.concatenate([ff_pack[:down_lines], swap.reshape(-1, 128)], axis=0)
    ff_gathered = lax.all_gather(ff_pack, SEQ, axis=0)
    d_normed = mm_nt(d_queries, query_w) + mm_nt(d_latent, latent_w)
    tokens_grad = (d_resid + norm_pull(tok, inv_one, gain_one, d_normed)).astype(BF16)
    block = []
    for i in range(ndp):
        parts = [x[i * chunk[1] * strip : (i + 1) * chunk[1] * strip] for x, chunk in zip(out_parts, chunks)]
        block.append(jnp.concatenate([parts[j] for j in order_of]))
    layer_out = (resid + scatter_dp(block)).astype(BF16)

    grad_pack = scatter_dp(chip_parts).astype(BF16)
    own, ff_gathered = together(grad_pack, ff_gathered)
    own = own.reshape(nz, -1, width)
    down_out, gate_out, up_out, gain_two_sum = unpack_ff(
        ff_gathered, w_gate, w_up, slice_ff, width, own_rows, down_rows
    )
    own = lax.psum_scatter(own, "z", scatter_dimension=0, tiled=True)
    own, gain_two_sum = together(own[0], gain_two_sum)
    own = lax.all_gather(own, SEQ, axis=0).reshape(nz, 2, -1, width)
    lat_rows = half * lat_width // width
    sections = (half, up_half, up_half, half, lat_rows)
    if own.shape[2] % 32 == 0:
        query_out, key_out, value_out, out_out, latent_out, gain_one_sum = unpack_attention(
            own, w_query, w_latent, sections
        )
    else:
        own = own.transpose(1, 0, 2, 3).reshape(2, -1, width).astype(F32)
        query_out, key_out, value_out, out_out, latent_out = (
            own[:, cut : cut + count].reshape(-1, width) for cut, count in zip([*cuts[:-1], cuts[-1]], sections)
        )
        fold = width // lat_width
        latent_out = latent_out.reshape(2, lat_rows, fold, lat_width).transpose(0, 2, 1, 3).reshape(shard, lat_width)
        gain_one_sum = jnp.sum(w_query.astype(F32) * query_out, axis=1, keepdims=True)
        gain_one_sum += jnp.sum(w_latent.astype(F32) * latent_out, axis=1, keepdims=True)

    gain_one_out = gain_one_sum[:, 0] / norm1_gain.astype(F32)
    gain_two_out = gain_two_sum[:, 0] / norm2_gain.astype(F32)

    shape = (1, pieces, strip, width)
    return (
        layer_out.reshape(shape), tokens_grad.reshape(shape), gain_one_out, query_out, latent_out, key_out,
        value_out, out_out, gain_two_out, gate_out, up_out, down_out,
    )


def solution(mesh):
    sizes = mesh.shape
    grid = Mesh(mesh.devices.reshape(sizes["dp"], sizes["seq"] // 2, 2), ("dp", "z", "core"))
    stream = P("dp", None, SEQ, None)
    vector, matrix = P("dp"), P("dp", None)
    in_specs = (
        stream, vector, matrix, matrix, matrix, matrix, matrix, vector, matrix, matrix, matrix, stream, matrix,
    )
    out_specs = (
        stream, stream, vector, matrix, matrix, matrix, matrix, matrix, vector, matrix, matrix, matrix,
    )
    return jax.shard_map(per_device, mesh=grid, in_specs=in_specs, out_specs=out_specs, check_vma=False)
```

```python
import functools
import math

import jax
import jax.numpy as jnp
from jax import lax
from jax.experimental import pallas as pl
from jax.experimental.pallas import tpu as pltpu
from jax.sharding import Mesh
from jax.sharding import PartitionSpec as P

HEADS = 16
HEAD_DIM = 64
GROUPS = 2
LATENT = 256
PER_GROUP = HEADS // GROUPS
GROUP_COLS = PER_GROUP * HEAD_DIM
KEY_BLOCK = 256
VMEM_FORWARD = 56
VMEM_BACKWARD = 56
SCALE = 1.0 / math.sqrt(HEAD_DIM)
NEG_FILL = -1e30
NORM_EPS = 1e-05
F32 = jnp.float32
BF16 = jnp.bfloat16
DP = "dp"
SEQ = ("z", "core")
NO_COST = pl.CostEstimate(flops=0, transcendentals=0, bytes_accessed=0)
CHIP = ("dp", "core")


def mm(a, b):
    return jnp.dot(a, b, preferred_element_type=F32)


def mm_nt(a, b):
    return lax.dot_general(a, b, (((1,), (1,)), ((), ())), preferred_element_type=F32)


def mm_tn(a, b):
    return lax.dot_general(a, b, (((0,), (0,)), ((), ())), preferred_element_type=F32)


def low_lanes(rows):
    return lax.broadcasted_iota(jnp.int32, (rows, 2 * HEAD_DIM), 1) < HEAD_DIM


def pair_cols(pair):
    return slice(2 * HEAD_DIM * pair, 2 * HEAD_DIM * (pair + 1))


def expand_pair(part, proj):
    low = low_lanes(part.shape[0])
    zero = jnp.zeros_like(part)
    both = jnp.concatenate([jnp.where(low, part, zero), jnp.where(low, zero, part)], axis=0)
    return mm_nt(both, proj)


def shrink_pair(parts, proj):
    rows = parts.shape[0] // 2
    both = mm(parts, proj)
    return jnp.where(low_lanes(rows), both[:rows], both[rows:])


def outer_pair(parts, vals):
    rows = vals.shape[0]
    return jnp.where(low_lanes(LATENT), mm_tn(parts[:rows], vals), mm_tn(parts[rows:], vals))


def load_keys(lat_ref, slot_ref, block, strips, per_piece):
    piece = block // per_piece
    first = (block - piece * per_piece) * strips
    parts = [lat_ref[slot_ref[first + i], piece] for i in range(strips)]
    return jnp.concatenate(parts, axis=0), piece, first


def visible(block, base, starts, rows):
    key_pos = block * KEY_BLOCK + lax.broadcasted_iota(jnp.int32, (KEY_BLOCK, 2 * rows), 0)
    row_pos = base + lax.broadcasted_iota(jnp.int32, (KEY_BLOCK, 2 * rows), 1) % rows
    return (key_pos >= starts) & (key_pos <= row_pos)


def masked(scores, seen):
    wide = seen.shape[1]
    parts = [
        jnp.where(seen, scores[:, i * wide : (i + 1) * wide], NEG_FILL) for i in range(scores.shape[1] // wide)
    ]
    return jnp.concatenate(parts, axis=1)


def copies(sources, target_ref, sem):
    return [
        pltpu.make_async_copy(source, target_ref.at[slot], sem.at[slot]) for slot, source in enumerate(sources)
    ]


def latent_cols(group):
    return slice(group * LATENT, (group + 1) * LATENT)


def forward_body(first_piece, nseq, waits, lo_ref, hi_ref, base_ref, slot_ref, *refs):
    sources, refs = refs[:nseq], refs[nseq + waits :]
    start_ref, query_ref, key_up_ref, value_up_ref = refs[:4]
    abs_ref, mixed_ref, lse_ref, out_ref, top_ref, sum_ref, acc_ref, lat_ref, lat_sem = refs[4:]
    fetches = copies(sources, lat_ref, lat_sem)
    for fetch in fetches:
        fetch.start()
    strip = lat_ref.shape[2]
    groups, _, count = mixed_ref.shape[:3]
    strips = KEY_BLOCK // strip
    per_piece = nseq // strips
    tall = PER_GROUP * strip
    pairs = PER_GROUP // 2
    for pair in range(groups * pairs):
        cols = pair_cols(pair)
        part = expand_pair(query_ref[:, cols], key_up_ref[:, cols])
        part = part.astype(BF16) * jnp.asarray(SCALE, BF16)
        first = 2 * (pair % pairs)
        abs_ref[pair // pairs, first : first + 2] = part.reshape(2, count, strip, LATENT)
    for fetch in fetches:
        fetch.wait()

    for index in range(count):
        piece_id = index + first_piece
        top_ref[...] = jnp.full(top_ref.shape, NEG_FILL, F32)
        sum_ref[...] = jnp.zeros(sum_ref.shape, F32)
        acc_ref[...] = jnp.zeros(acc_ref.shape, F32)
        starts = jnp.broadcast_to(start_ref[index, 0:1], (KEY_BLOCK, 2 * strip))

        def step(block, carry):
            keys, _, _ = load_keys(lat_ref, slot_ref, block, strips, per_piece)
            keys = [keys[:, latent_cols(g)] for g in range(groups)]
            seen = visible(block, base_ref[piece_id], starts, strip)
            tops = [top_ref[g] for g in range(groups)]
            sums = [sum_ref[g] for g in range(groups)]
            raw = [mm_nt(keys[g], abs_ref[g, :, index].reshape(tall, LATENT)) for g in range(groups)]
            done = []
            for g in range(groups):
                scores = masked(raw[g], seen)
                new_top = jnp.maximum(tops[g], jnp.max(scores, axis=0, keepdims=True))
                shrink = jnp.exp(tops[g] - new_top)
                probs = jnp.exp(scores - new_top)
                total = sums[g] * shrink + jnp.sum(probs, axis=0, keepdims=True)
                done.append((new_top, total, shrink, mm_tn(keys[g], probs.astype(BF16))))
            for g in range(groups):
                new_top, total, shrink, term = done[g]
                top_ref[g] = new_top
                sum_ref[g] = total
                acc_ref[g] = acc_ref[g] * shrink + term
            return carry

        lax.fori_loop(lo_ref[piece_id], hi_ref[piece_id], step, 0)
        for g in range(groups):
            total = sum_ref[g]
            lse_ref[g, index] = jnp.broadcast_to(top_ref[g] + jnp.log(total), (8, tall))
            mixed = (acc_ref[g] * (1.0 / total)).T.astype(BF16)
            mixed_ref[g, :, index] = mixed.reshape(PER_GROUP, strip, LATENT)

    for pair in range(groups * pairs):
        cols = pair_cols(pair)
        first = 2 * (pair % pairs)
        parts = mixed_ref[pair // pairs, first : first + 2].reshape(2 * count * strip, LATENT)
        out_ref[:, cols] = shrink_pair(parts, value_up_ref[:, cols]).astype(BF16)


def backward_body(nseq, waits, lo_ref, hi_ref, base_ref, slot_ref, place_ref, *refs):
    sources, refs = refs[:nseq], refs[nseq + waits :]
    start_ref, query_ref, key_up_ref, value_up_ref, normed_ref, out_ref, resid_grad_ref, normed_hbm = refs[:8]
    abs_front, abs_back, mixed_front, mixed_back, lse_front, lse_back, grad_ref = refs[8:15]
    dquery_ref, dlat_hbm, mine_ref, theirs_ref = refs[15:19]
    dmix_ref, delta_ref, acc_ref, dabs_ref, dkey_ref, latent_sum_ref, stage_ref, lat_ref, lat_sem = refs[19:28]
    stream_ref, stream_sem, dlat_sem = refs[28:]
    fetches = copies(sources, lat_ref, lat_sem)
    for fetch in fetches:
        fetch.start()
    _, pieces, strip, _ = lat_ref.shape
    groups, _, cut = mixed_front.shape[:3]
    strips = KEY_BLOCK // strip
    per_piece = nseq // strips
    tall = PER_GROUP * strip
    pairs = PER_GROUP // 2
    depth = stream_ref.shape[0]
    my_core, my_dp = place_ref[0], place_ref[1]
    ndp = mine_ref.shape[0]

    def fetch_stream(seq):
        slot = seq % depth
        return pltpu.make_async_copy(normed_hbm.at[seq], stream_ref.at[slot], stream_sem.at[slot])

    for seq in range(depth):
        fetch_stream(seq).start()

    def give(first, grad):
        rows = grad.shape[0] // (2 * ndp)
        for dp in range(ndp):
            for core in range(2):
                part = grad[(2 * dp + core) * rows : (2 * dp + core + 1) * rows]

                @pl.when(my_core == core)
                def _():
                    mine_ref[dp ^ my_dp, first : first + rows] = part

                @pl.when(my_core != core)
                def _():
                    theirs_ref[dp ^ my_dp, first : first + rows] = part

    def of_pair(g, first):
        parts = [ref[g, first : first + 2] for ref in (mixed_front, mixed_back)]
        return jnp.concatenate(parts, axis=1).reshape(2 * pieces * strip, LATENT)

    def clear(slot, carry):
        dkey_ref[slot] = jnp.zeros(dkey_ref.shape[1:], F32)
        return carry

    lax.fori_loop(0, nseq, clear, 0)
    for pair in range(groups * pairs):
        cols = pair_cols(pair)
        g, first = pair // pairs, 2 * (pair % pairs)
        grads = grad_ref[:, cols]
        part = expand_pair(grads, value_up_ref[:, cols]).astype(BF16)
        dmix_ref[g, first : first + 2] = part.reshape(2, pieces, strip, LATENT)
        stage_ref[0, :, cols] = outer_pair(of_pair(g, first), grads).astype(BF16)
    for fetch in fetches:
        fetch.wait()

    for piece_id in range(pieces):
        index = piece_id if piece_id < cut else piece_id - cut
        front = piece_id < cut
        abs_ref, mixed_ref, lse_ref = (
            (abs_front, mixed_front, lse_front) if front else (abs_back, mixed_back, lse_back)
        )
        for g in range(groups):
            dmix_all = dmix_ref[g, :, piece_id].reshape(tall, LATENT).astype(F32)
            mixed_all = mixed_ref[g, :, index].reshape(tall, LATENT).astype(F32)
            delta = jnp.sum(dmix_all * mixed_all, axis=1, keepdims=True)
            delta_ref[g] = jnp.broadcast_to(delta, (tall, 128)).T[:8]
        acc_ref[...] = jnp.zeros(acc_ref.shape, F32)
        starts = jnp.broadcast_to(start_ref[piece_id, 0:1], (KEY_BLOCK, 2 * strip))

        def step(block, carry):
            keys, key_piece, first = load_keys(lat_ref, slot_ref, block, strips, per_piece)
            keys = [keys[:, latent_cols(g)] for g in range(groups)]
            seen = visible(block, base_ref[piece_id], starts, strip)
            absorbed = [abs_ref[g, :, index].reshape(tall, LATENT) for g in range(groups)]
            dmix = [dmix_ref[g, :, piece_id].reshape(tall, LATENT) for g in range(groups)]
            raw = [(mm_nt(keys[g], absorbed[g]), mm_nt(keys[g], dmix[g])) for g in range(groups)]
            done = []
            for g in range(groups):
                probs = jnp.exp(masked(raw[g][0] - lse_ref[g, index, 0:1], seen))
                d_scores = (probs * (raw[g][1] - delta_ref[g, 0:1])).astype(BF16)
                d_keys = mm(d_scores, absorbed[g]) + mm(probs.astype(BF16), dmix[g])
                done.append((mm_tn(d_scores, keys[g]), d_keys))
            for g in range(groups):
                acc_ref[g] += done[g][0]
                for i in range(strips):
                    part = done[g][1][i * strip : (i + 1) * strip]
                    dkey_ref[slot_ref[first + i], key_piece, :, latent_cols(g)] += part
            return carry

        lax.fori_loop(lo_ref[piece_id], hi_ref[piece_id], step, 0)
        for g in range(groups):
            dabs_ref[g, :, piece_id] = (acc_ref[g] * SCALE).astype(BF16).reshape(PER_GROUP, strip, LATENT)

    def settle(slot, carry):
        lat_ref[slot] = dkey_ref[slot].astype(BF16)
        return carry

    lax.fori_loop(0, nseq, settle, 0)
    send = pltpu.make_async_copy(lat_ref, dlat_hbm, dlat_sem)
    send.start()
    for pair in range(groups * pairs):
        cols = pair_cols(pair)
        g, first = pair // pairs, 2 * (pair % pairs)
        parts = dabs_ref[g, first : first + 2].reshape(2 * pieces * strip, LATENT)
        dquery_ref[:, cols] = shrink_pair(parts, key_up_ref[:, cols]).astype(BF16)
        stage_ref[1, :, cols] = outer_pair(parts, query_ref[:, cols]).astype(BF16)

    width = normed_ref.shape[1]
    half = width // (2 * ndp)
    up_half = LATENT // (2 * ndp)
    give(0, mm_tn(normed_ref[...], dquery_ref[...]).astype(BF16))
    give(half, stage_ref[1])
    give(half + up_half, stage_ref[0])
    give(half + 2 * up_half, mm_tn(out_ref[...], resid_grad_ref[...]).astype(BF16))
    latent_sum_ref[...] = jnp.zeros(latent_sum_ref.shape, F32)

    def latent_term(seq, carry):
        fetch_stream(seq).wait()
        rows = stream_ref[seq % depth].reshape(pieces * strip, width)
        grads = lat_ref[slot_ref[seq]].reshape(pieces * strip, groups * LATENT)
        latent_sum_ref[...] += mm_tn(rows, grads)

        @pl.when(seq + depth < nseq)
        def _():
            fetch_stream(seq + depth).start()

        return carry

    lax.fori_loop(0, nseq, latent_term, 0)
    lat_width = groups * LATENT
    fold = width // lat_width
    latent_grad = latent_sum_ref[...].astype(BF16).reshape(2 * ndp, fold, half // fold, lat_width)
    latent_grad = [latent_grad[:, i].reshape(width // fold, lat_width) for i in range(fold)]
    give(2 * half + 2 * up_half, jnp.concatenate(latent_grad, axis=1))
    send.wait()


def attention_specs(strip, pieces):
    tall = PER_GROUP * strip

    def whole(*shape):
        return pl.BlockSpec(shape, lambda *_: (0,) * len(shape), pipeline_mode=pl.Buffered(1))

    table = whole(pieces, 8, 2 * strip)
    rows = whole(pieces * strip, GROUPS * GROUP_COLS)
    proj = whole(LATENT, GROUPS * GROUP_COLS)
    heads = whole(GROUPS, PER_GROUP, pieces, strip, LATENT)
    lse = whole(GROUPS, pieces, 8, tall)
    return whole, table, rows, proj, heads, lse


def kernel_params(vmem):
    return pltpu.CompilerParams(dimension_semantics=("arbitrary",), vmem_limit_bytes=vmem << 20)


def attention_forward(first_piece, pieces, tables, table, latents, queries, key_up, value_up, waits):
    nseq = len(latents)
    strip = latents[0].shape[1]
    tall = PER_GROUP * strip
    _, t_spec, row_spec, proj_spec, head_spec, lse_spec = attention_specs(strip, pieces)
    head_shape = jax.ShapeDtypeStruct((GROUPS, PER_GROUP, pieces, strip, LATENT), BF16)
    in_place = pl.BlockSpec(memory_space=pl.ANY)
    return pl.pallas_call(
        functools.partial(forward_body, first_piece, nseq, len(waits)),
        name="attention_forward",
        grid_spec=pltpu.PrefetchScalarGridSpec(
            num_scalar_prefetch=len(tables),
            grid=(1,),
            in_specs=[in_place] * (nseq + len(waits)) + [t_spec, row_spec, proj_spec, proj_spec],
            out_specs=[head_spec, head_spec, lse_spec, row_spec],
            scratch_shapes=[
                pltpu.VMEM((GROUPS, 1, tall), F32),
                pltpu.VMEM((GROUPS, 1, tall), F32),
                pltpu.VMEM((GROUPS, LATENT, tall), F32),
                pltpu.VMEM((nseq, *latents[0].shape), BF16),
                pltpu.SemaphoreType.DMA((nseq,)),
            ],
        ),
        out_shape=[
            head_shape,
            head_shape,
            jax.ShapeDtypeStruct((GROUPS, pieces, 8, tall), F32),
            jax.ShapeDtypeStruct((pieces * strip, queries.shape[1]), BF16),
        ],
        compiler_params=kernel_params(VMEM_FORWARD if nseq <= 8 else 56),
        cost_estimate=NO_COST,
    )(*tables, *latents, *waits, table, queries, key_up, value_up)


def attention_backward(
    tables, place, latents, table, queries, key_up, value_up, normed, heads_out, resid_grads, normed_stream,
    absorbed, mixed, lse, grads, ndp, waits,
):
    nseq = len(latents)
    pieces, strip, lat_width = latents[0].shape
    tall = PER_GROUP * strip
    cut = mixed[0].shape[2]
    whole, t_spec, row_spec, proj_spec, _, _ = attention_specs(strip, pieces)
    head_front, lse_front = attention_specs(strip, cut)[4:]
    head_back, lse_back = attention_specs(strip, pieces - cut)[4:]
    width = normed_stream.shape[3]
    depth = nseq if nseq <= 8 else 2
    part = (ndp, (2 * width + 2 * LATENT + lat_width * width // key_up.shape[1]) // (2 * ndp), width)
    in_place = pl.BlockSpec(memory_space=pl.ANY)
    return pl.pallas_call(
        functools.partial(backward_body, nseq, len(waits)),
        name="attention_backward",
        grid_spec=pltpu.PrefetchScalarGridSpec(
            num_scalar_prefetch=len(tables) + 1,
            grid=(1,),
            in_specs=[in_place] * (nseq + len(waits)) + [
                t_spec, row_spec, proj_spec, proj_spec, row_spec, row_spec, row_spec, in_place,
                head_front, head_back, head_front, head_back, lse_front, lse_back, row_spec,
            ],
            out_specs=[row_spec, in_place, whole(*part), whole(*part)],
            scratch_shapes=[
                pltpu.VMEM((GROUPS, PER_GROUP, pieces, strip, LATENT), BF16),
                pltpu.VMEM((GROUPS, 8, tall), F32),
                pltpu.VMEM((GROUPS, tall, LATENT), F32),
                pltpu.VMEM((GROUPS, PER_GROUP, pieces, strip, LATENT), BF16),
                pltpu.VMEM((nseq, pieces, strip, lat_width), F32),
                pltpu.VMEM((width, lat_width), F32),
                pltpu.VMEM((2, LATENT, GROUPS * GROUP_COLS), BF16),
                pltpu.VMEM((nseq, pieces, strip, lat_width), BF16),
                pltpu.SemaphoreType.DMA((nseq,)),
                pltpu.VMEM((depth, *normed_stream.shape[1:]), BF16),
                pltpu.SemaphoreType.DMA((depth,)),
                pltpu.SemaphoreType.DMA,
            ],
        ),
        out_shape=[
            jax.ShapeDtypeStruct(queries.shape, BF16),
            jax.ShapeDtypeStruct((nseq, pieces, strip, lat_width), BF16),
            jax.ShapeDtypeStruct(part, BF16),
            jax.ShapeDtypeStruct(part, BF16),
        ],
        compiler_params=kernel_params(VMEM_BACKWARD if nseq <= 8 else 62),
        cost_estimate=NO_COST,
    )(
        *tables, place, *latents, *waits, table, queries, key_up, value_up, normed, heads_out, resid_grads, normed_stream,
        *absorbed, *mixed, *lse, grads,
    )


def positions_body(pieces, nz, strip, place_ref, lengths_ref, table_ref, lo_ref, hi_ref, base_ref, slot_ref):
    my_core, my_z = place_ref[0], place_ref[2]
    span = strip * 2 * nz
    mine = (2 * my_z + my_core) * strip
    wide = table_ref.shape[2]
    lane = lax.broadcasted_iota(jnp.int32, (1, wide), 1) % strip
    positions = [piece * span + mine + lane for piece in range(pieces)]
    ids = [piece * span + mine for piece in range(pieces)]

    def entry(i, carry):
        first, starts, lows = carry
        end = first + lengths_ref[0, 2 * i]
        starts = [jnp.where((p >= first) & (p < end), first, s) for p, s in zip(positions, starts)]
        lows = [jnp.where((p >= first) & (p < end), first, s) for p, s in zip(ids, lows)]
        return end + lengths_ref[0, 2 * i + 1], starts, lows

    _, starts, lows = lax.fori_loop(0, lengths_ref.shape[1] // 2, entry, (jnp.int32(0), positions, ids))
    for piece in range(pieces):
        table_ref[piece] = jnp.broadcast_to(starts[piece], table_ref.shape[1:])
        lo_ref[piece] = lows[piece] // KEY_BLOCK
        hi_ref[piece] = (ids[piece] + strip + KEY_BLOCK - 1) // KEY_BLOCK
        base_ref[piece] = ids[piece]
    for seq in range(2 * nz):
        core = jnp.where(my_core == seq % 2, 0, 1)
        slot_ref[seq] = core * nz + jnp.where(my_z >= seq // 2, my_z - seq // 2, my_z - seq // 2 + nz)


def positions_of(place, lengths, pieces, nz, strip):
    small = pl.BlockSpec(memory_space=pltpu.SMEM)
    counts = [pieces, pieces, pieces, 2 * nz]
    table, *tables = pl.pallas_call(
        functools.partial(positions_body, pieces, nz, strip),
        name="positions",
        grid_spec=pltpu.PrefetchScalarGridSpec(
            num_scalar_prefetch=1,
            grid=(1,),
            in_specs=[small],
            out_specs=[whole_spec(pieces, 8, 2 * strip)] + [small] * 4,
        ),
        out_shape=[jax.ShapeDtypeStruct((pieces, 8, 2 * strip), jnp.int32)]
        + [jax.ShapeDtypeStruct((count,), jnp.int32) for count in counts],
        cost_estimate=NO_COST,
    )(place, lengths)
    return table, tuple(tables)


def cut_body(place_ref, gate_hbm, up_hbm, out_ref, rows_ref, sems):
    ndp, _, half, wide = out_ref.shape
    first = pl.multiple_of(place_ref[0] * half, half)
    fetches = [
        pltpu.make_async_copy(source.at[pl.ds(first, half)], rows_ref.at[i], sems.at[i])
        for i, source in enumerate((gate_hbm, up_hbm))
    ]
    for fetch in fetches:
        fetch.start()
    slice_ff = gate_hbm.shape[1] // ndp
    low = lax.broadcasted_iota(jnp.int32, (half, 128), 1) < 64
    zero = jnp.zeros((half, 128), F32)
    whole_tiles = slice_ff // 128
    for which, fetch in enumerate(fetches):
        fetch.wait()

        def tile_of(t):
            return rows_ref[which, :, t * 128 : (t + 1) * 128].astype(F32)

        for dp in range(ndp):
            first_tile = dp * slice_ff // 128
            if dp % 2 == 0:
                parts = [tile_of(first_tile + t) for t in range(whole_tiles)]
                parts.append(jnp.where(low, tile_of(first_tile + whole_tiles), zero))
            else:
                halves = [pltpu.roll(tile_of(first_tile + t), 64, 1) for t in range(whole_tiles + 1)]
                parts = [jnp.where(low, halves[t], halves[t + 1]) for t in range(whole_tiles)]
                parts.append(jnp.where(low, halves[whole_tiles], zero))
            for t, part in enumerate(parts):
                out_ref[dp, which, :, t * 128 : (t + 1) * 128] = part.astype(BF16)


def cut_columns(place, w_gate, w_up, ndp, half):
    ff = w_gate.shape[1]
    wide = -(-ff // ndp // 128) * 128
    in_place = pl.BlockSpec(memory_space=pl.ANY)
    return pl.pallas_call(
        cut_body,
        name="cut_columns",
        grid_spec=pltpu.PrefetchScalarGridSpec(
            num_scalar_prefetch=1,
            grid=(1,),
            in_specs=[in_place, in_place],
            out_specs=whole_spec(ndp, 2, half, wide),
            scratch_shapes=[pltpu.VMEM((2, half, ff), BF16), pltpu.SemaphoreType.DMA((2,))],
        ),
        out_shape=jax.ShapeDtypeStruct((ndp, 2, half, wide), BF16),
        compiler_params=kernel_params(16),
        cost_estimate=NO_COST,
    )(place, w_gate, w_up)


def front_body(ndp, place_ref, tok_ref, *refs):
    blocks, refs = refs[:ndp], refs[ndp:]
    other_hbm, normed_ref, latent_ref, gain_out_ref, weight_ref, gain_ref, sems = refs
    my_core, my_dp = place_ref[0], place_ref[1]
    half = other_hbm.shape[1] - 16
    width = tok_ref.shape[1]
    shard = 2 * half
    fetches = []
    for i in range(ndp):
        dp = my_dp ^ i
        for core, source in enumerate((blocks[i], other_hbm.at[i])):
            first = pl.multiple_of(dp * shard + (my_core ^ core) * half, half)
            fetches.append((source.at[pl.ds(0, half)], weight_ref.at[pl.ds(first, half)]))
        fetches.append((blocks[i].at[pl.ds(half, 16)], gain_ref.at[dp]))
    fetches = [pltpu.make_async_copy(a, b, sems.at[i]) for i, (a, b) in enumerate(fetches)]
    for fetch in fetches:
        fetch.start()
    tok = tok_ref[...].astype(F32)
    scaled = tok * inverse_rms(tok)
    for fetch in fetches:
        fetch.wait()
    gains = [gain_ref[dp].astype(F32) for dp in range(ndp)]
    gain_one = jnp.concatenate([g[0:1, :shard] for g in gains], axis=1)
    gain_two = jnp.concatenate([g[0:1, shard : 2 * shard] for g in gains], axis=1)
    normed = (scaled * gain_one).astype(BF16)
    normed_ref[...] = normed
    latent_ref[...] = mm(normed, weight_ref[...]).astype(BF16)
    gain_out_ref[0:8] = jnp.broadcast_to(gain_one, (8, width))
    gain_out_ref[8:16] = jnp.broadcast_to(gain_two, (8, width))


def front(place, tok, blocks, other):
    rows, width = tok.shape
    ndp = len(blocks)
    lat_width = other.shape[2]
    in_place = pl.BlockSpec(memory_space=pl.ANY)
    return pl.pallas_call(
        functools.partial(front_body, ndp),
        name="front",
        grid_spec=pltpu.PrefetchScalarGridSpec(
            num_scalar_prefetch=1,
            grid=(1,),
            in_specs=[whole_spec(rows, width)] + [in_place] * (ndp + 1),
            out_specs=[
                whole_spec(rows, width), whole_spec(rows, lat_width), whole_spec(16, width),
                whole_spec(width, lat_width),
            ],
            scratch_shapes=[
                pltpu.VMEM((ndp, 16, lat_width), BF16),
                pltpu.SemaphoreType.DMA((3 * ndp,)),
            ],
        ),
        out_shape=[
            jax.ShapeDtypeStruct((rows, width), BF16),
            jax.ShapeDtypeStruct((rows, lat_width), BF16),
            jax.ShapeDtypeStruct((16, width), F32),
            jax.ShapeDtypeStruct((width, lat_width), BF16),
        ],
        compiler_params=kernel_params(16),
        cost_estimate=NO_COST,
    )(place, tok, *blocks, other)


def ff_body(ndp, first_row, waits, place_ref, *refs):
    blocks, refs = refs[:ndp], refs[ndp + waits :]
    grad_hbm, mine_hbm, theirs_hbm, down_hbm = refs[:4]
    hidden_ref, dgate_ref, dup_ref = refs[4:7]
    part_refs, refs = refs[7 : 7 + ndp], refs[7 + ndp :]
    weight_ref, down_ref, grad_ref, weight_sem, down_sem, grad_sem = refs
    my_core, my_dp = place_ref[0], place_ref[1]
    size, width = blocks[0].shape
    slice_ff = down_hbm.shape[0]
    wide = hidden_ref.shape[1]
    half = mine_hbm.shape[2]
    fetch_down = pltpu.make_async_copy(down_hbm, down_ref.at[pl.ds(0, slice_ff)], down_sem)
    fetch_down.start()
    fetch_grads = [
        pltpu.make_async_copy(
            grad_hbm.at[my_dp ^ i, pl.ds(first_row, size)], grad_ref.at[pl.ds(i * size, size)], grad_sem.at[i]
        )
        for i in range(ndp)
    ]
    for fetch in fetch_grads:
        fetch.start()
    fetch_weights = []
    for which in range(2):
        for dp in range(ndp):
            for core, source in enumerate((mine_hbm, theirs_hbm)):
                first = pl.multiple_of((2 * dp + (my_core ^ core)) * half, half)
                fetch_weights.append(
                    pltpu.make_async_copy(
                        source.at[dp, which], weight_ref.at[which, pl.ds(first, half)],
                        weight_sem.at[which, 2 * dp + core],
                    )
                )
    for fetch in fetch_weights:
        fetch.start()
    if wide > slice_ff:
        down_ref[slice_ff:] = jnp.zeros((wide - slice_ff, width), BF16)
    fetch_down.wait()
    for fetch in fetch_grads + fetch_weights:
        fetch.wait()
    per = max(ndp // 2, 1)
    for first in range(0, ndp, per):
        span = slice(first * size, (first + per) * size)
        normed = jnp.concatenate([blocks[i][...] for i in range(first, first + per)], axis=0)
        gate = mm(normed, weight_ref[0])
        up = mm(normed, weight_ref[1])
        d_hidden = mm_nt(grad_ref[span], down_ref[...])
        sig = 1.0 / (1.0 + jnp.exp(-gate))
        silu = gate * sig
        hidden_ref[span] = (silu * up).astype(BF16)
        d_gate = (d_hidden * up * (sig * (1.0 + gate * (1.0 - sig)))).astype(BF16)
        d_up = (d_hidden * silu).astype(BF16)
        dgate_ref[span] = d_gate
        dup_ref[span] = d_up
        part = (mm_nt(d_gate, weight_ref[0]) + mm_nt(d_up, weight_ref[1])).astype(BF16)
        for i in range(per):
            part_refs[first + i][...] = part[i * size : (i + 1) * size]


def whole_spec(*shape):
    return pl.BlockSpec(shape, lambda *_: (0,) * len(shape), pipeline_mode=pl.Buffered(1))


def feed_forward(place, first_row, blocks, grad_blocks, mine, theirs, down, waits):
    ndp = len(blocks)
    size, width = blocks[0].shape
    wide = mine.shape[3]
    in_place = pl.BlockSpec(memory_space=pl.ANY)
    tall = jax.ShapeDtypeStruct((ndp * size, wide), BF16)
    return pl.pallas_call(
        functools.partial(ff_body, ndp, first_row, len(waits)),
        name="feed_forward",
        grid_spec=pltpu.PrefetchScalarGridSpec(
            num_scalar_prefetch=1,
            grid=(1,),
            in_specs=[whole_spec(size, width)] * ndp + [in_place] * (len(waits) + 4),
            out_specs=[whole_spec(ndp * size, wide)] * 3 + [whole_spec(size, width)] * ndp,
            scratch_shapes=[
                pltpu.VMEM((2, width, wide), BF16),
                pltpu.VMEM((wide, width), BF16),
                pltpu.VMEM((ndp * size, width), BF16),
                pltpu.SemaphoreType.DMA((2, 2 * ndp)),
                pltpu.SemaphoreType.DMA,
                pltpu.SemaphoreType.DMA((ndp,)),
            ],
        ),
        out_shape=[tall] * 3 + [jax.ShapeDtypeStruct((size, width), BF16)] * ndp,
        compiler_params=kernel_params(48),
        cost_estimate=NO_COST,
    )(place, *blocks, *waits, grad_blocks, mine, theirs, down)


def ff_grad_body(ndp, nseq, spans, owned, waits, place_ref, *refs):
    blocks, refs = refs[: ndp * len(spans)], refs[ndp * len(spans) + waits :]
    sides, refs = refs[: 3 * len(spans)], refs[3 * len(spans) :]
    grad_hbm, pack_ref, normed_ref, grad_ref, hidden_ref, dgate_ref, dup_ref, sems = refs
    my_dp = place_ref[1]
    width = normed_ref.shape[1]
    wide = hidden_ref.shape[1]
    down_rows, own_rows = owned
    fetches = []

    def fetch(source, target):
        copy = pltpu.make_async_copy(source, target, sems.at[len(fetches)])
        copy.start()
        fetches.append(copy)

    row = 0
    for chunk, (first_row, size) in enumerate(spans):
        for target, source in zip((hidden_ref, dgate_ref, dup_ref), sides[3 * chunk : 3 * chunk + 3]):
            fetch(source, target.at[pl.ds(row, ndp * size)])
        for i in range(ndp):
            fetch(blocks[ndp * chunk + i], normed_ref.at[pl.ds(row + i * size, size)])
            fetch(grad_hbm.at[my_dp ^ i, pl.ds(first_row, size)], grad_ref.at[pl.ds(row + i * size, size)])
        row += ndp * size
    for copy in fetches:
        copy.wait()

    def give(seq, first, part):
        rows = part.shape[0]
        for tile in range(part.shape[1] // 128):
            pack_ref[seq, first + tile * rows : first + (tile + 1) * rows] = part[:, tile * 128 : (tile + 1) * 128]

    some = wide // 2
    for first in range(0, wide, some):
        part = mm_tn(hidden_ref[:, first : first + some], grad_ref[...]).astype(BF16)
        for i in range(some // down_rows):
            give(first // down_rows + i, 0, part[i * down_rows : (i + 1) * down_rows])
    for seq in range(wide // down_rows, nseq):
        give(seq, 0, jnp.zeros((down_rows, width), BF16))
    shard = width // ndp
    first = down_rows * width // 128
    for dp in range(ndp):
        for side in (dgate_ref, dup_ref):
            part = mm_tn(normed_ref[:, dp * shard : (dp + 1) * shard], side[...]).astype(BF16)
            for seq in range(nseq):
                if seq * own_rows < shard:
                    give(seq, first, part[seq * own_rows : (seq + 1) * own_rows])
                else:
                    give(seq, first, jnp.zeros((own_rows, wide), BF16))
            first += own_rows * wide // 128


def ff_gradients(place, spans, blocks, sides, grad_blocks, nseq, owned, waits):
    ndp = len(blocks) // len(spans)
    width = blocks[0].shape[1]
    wide = sides[0].shape[1]
    rows = ndp * sum(size for _, size in spans)
    down_rows, own_rows = owned
    pack = (nseq, (down_rows * width + 2 * ndp * own_rows * wide) // 128, 128)
    in_place = pl.BlockSpec(memory_space=pl.ANY)
    count = len(spans) * (3 + 2 * ndp)
    return pl.pallas_call(
        functools.partial(ff_grad_body, ndp, nseq, spans, owned, len(waits)),
        name="feed_forward_gradients",
        grid_spec=pltpu.PrefetchScalarGridSpec(
            num_scalar_prefetch=1,
            grid=(1,),
            in_specs=[in_place] * (len(blocks) + len(waits) + len(sides) + 1),
            out_specs=whole_spec(*pack),
            scratch_shapes=[
                pltpu.VMEM((rows, width), BF16),
                pltpu.VMEM((rows, width), BF16),
                pltpu.VMEM((rows, wide), BF16),
                pltpu.VMEM((rows, wide), BF16),
                pltpu.VMEM((rows, wide), BF16),
                pltpu.SemaphoreType.DMA((count,)),
            ],
        ),
        out_shape=jax.ShapeDtypeStruct(pack, BF16),
        compiler_params=kernel_params(48),
        cost_estimate=NO_COST,
    )(place, *blocks, *waits, *sides, grad_blocks)


def unpack_ff_body(ndp, own_rows, down_rows, pack_ref, gate_w_ref, up_w_ref, down_ref, gate_ref, up_ref, gain_ref):
    nseq = pack_ref.shape[0]
    slice_ff, width = down_ref.shape
    wide = -(-slice_ff // 128) * 128
    low = lax.broadcasted_iota(jnp.int32, (own_rows, 128), 1) < 64
    for seq in range(nseq):
        keep = min(down_rows, slice_ff - seq * down_rows)
        for tile in range(width // 128):
            if keep > 0:
                part = pack_ref[seq, tile * down_rows : (tile + 1) * down_rows].astype(F32)
                down_ref[seq * down_rows : seq * down_rows + keep, tile * 128 : (tile + 1) * 128] = part[:keep]
    for seq in range(gate_ref.shape[0] // own_rows):
        span = slice(seq * own_rows, (seq + 1) * own_rows)
        total = jnp.zeros((own_rows, 1), F32)
        for which, (out_ref, w_ref) in enumerate(((gate_ref, gate_w_ref), (up_ref, up_w_ref))):

            def tile_of(dp, tile):
                first = down_rows * width // 128 + ((2 * dp + which) * (wide // 128) + tile) * own_rows
                return pack_ref[seq, first : first + own_rows].astype(F32)

            whole_tiles = slice_ff // 128
            for dp in range(0, ndp, 2):
                first = dp * slice_ff // 128
                parts = [tile_of(dp, t) for t in range(whole_tiles)]
                halves = [pltpu.roll(tile_of(dp + 1, t), 64, 1) for t in range(whole_tiles + 1)]
                parts.append(jnp.where(low, tile_of(dp, whole_tiles), halves[0]))
                parts += [jnp.where(low, halves[t], halves[t + 1]) for t in range(whole_tiles)]
                for t, part in enumerate(parts):
                    cols = slice((first + t) * 128, (first + t + 1) * 128)
                    out_ref[span, cols] = part
                    total += jnp.sum(part * w_ref[span, cols].astype(F32), axis=1, keepdims=True)
        gain_ref[span] = jnp.broadcast_to(total, (own_rows, 128))


def unpack_ff(pack, w_gate, w_up, slice_ff, width, own_rows, down_rows):
    shard, ff = w_gate.shape
    full = jax.ShapeDtypeStruct((shard, ff), F32)
    return pl.pallas_call(
        functools.partial(unpack_ff_body, ff // slice_ff, own_rows, down_rows),
        name="unpack_feed_forward",
        grid=(1,),
        in_specs=[whole_spec(*pack.shape), whole_spec(shard, ff), whole_spec(shard, ff)],
        out_specs=[whole_spec(slice_ff, width), whole_spec(shard, ff), whole_spec(shard, ff), whole_spec(shard, 128)],
        out_shape=[
            jax.ShapeDtypeStruct((slice_ff, width), F32), full, full, jax.ShapeDtypeStruct((shard, 128), F32),
        ],
        compiler_params=kernel_params(40),
        cost_estimate=NO_COST,
    )(pack, w_gate, w_up)


def unpack_attention_body(
    sections, pack_ref, query_w_ref, latent_w_ref, query_ref, key_ref, value_ref, out_ref, latent_ref, gain_ref
):
    nz, _, rows, _ = pack_ref.shape
    step = 32
    for core in range(2):
        first = 0
        for section, target in zip(sections[:4], (query_ref, key_ref, value_ref, out_ref)):
            for row in range(0, section, step):
                place = first + row
                part = pack_ref[place // rows, core, place % rows : place % rows + step].astype(F32)
                target[core * section + row : core * section + row + step] = part
            first += section
        for row in range(0, sections[4], step):
            place = first + row
            part = pack_ref[place // rows, core, place % rows : place % rows + step].astype(F32)
            width = latent_ref.shape[1]
            for i in range(part.shape[1] // width):
                base = core * sections[0] + i * sections[4] + row
                latent_ref[base : base + step] = part[:, i * width : (i + 1) * width]
    total = jnp.sum(query_w_ref[...].astype(F32) * query_ref[...], axis=1, keepdims=True)
    total += jnp.sum(latent_w_ref[...].astype(F32) * latent_ref[...], axis=1, keepdims=True)
    gain_ref[...] = jnp.broadcast_to(total, gain_ref.shape)


def unpack_attention(pack, w_query, w_latent, sections):
    shard, width = w_query.shape
    lat_width = w_latent.shape[1]
    shapes = [
        (shard, width), (2 * sections[1], width), (2 * sections[2], width), (2 * sections[3], width),
        (shard, lat_width), (shard, 128),
    ]
    return pl.pallas_call(
        functools.partial(unpack_attention_body, sections),
        name="unpack_attention",
        grid=(1,),
        in_specs=[whole_spec(*pack.shape), whole_spec(shard, width), whole_spec(shard, lat_width)],
        out_specs=[whole_spec(*shape) for shape in shapes],
        out_shape=[jax.ShapeDtypeStruct(shape, F32) for shape in shapes],
        compiler_params=kernel_params(24),
        cost_estimate=NO_COST,
    )(pack, w_query, w_latent)


def inverse_rms(values):
    return lax.rsqrt(jnp.mean(values * values, axis=-1, keepdims=True) + NORM_EPS)


def norm_pull(values, inverse, gain, grads):
    scaled = gain * grads
    return inverse * scaled - values * (inverse**3) * jnp.mean(scaled * values, axis=-1, keepdims=True)


def my_half(shard):
    half = shard.shape[0] // 2
    return lax.dynamic_slice_in_dim(shard, lax.axis_index("core") * half, half, 0)


def swap_core(x):
    return lax.ppermute(x, "core", [(0, 1), (1, 0)])


def partner(x, step):
    return lax.ppermute(x, DP, [(i, i ^ step) for i in range(lax.axis_size(DP))])


def from_behind(x, step):
    nz = lax.axis_size("z")
    return lax.ppermute(x, "z", [(i, (i + step) % nz) for i in range(nz)])


def from_ahead(x, step):
    nz = lax.axis_size("z")
    return lax.ppermute(x, "z", [((i + step) % nz, i) for i in range(nz)])


def gather_dp(x):
    return [x] + [partner(x, step) for step in range(1, lax.axis_size(DP))]


def scatter_dp(parts):
    total = parts[0].astype(F32)
    for step in range(1, len(parts)):
        total = total + partner(parts[step].astype(BF16), step).astype(F32)
    return total


def together(*arrays):
    return lax.optimization_barrier(arrays)


def per_device(
    tokens, norm1_gain, w_query, w_latent, w_key_up, w_value_up, w_out, norm2_gain,
    w_gate, w_up, w_down, out_grad, seq_lengths,
):
    ndp = lax.axis_size(DP)
    nz = lax.axis_size("z")
    nseq = 2 * nz
    pieces, strip, width = tokens.shape[1:]
    rows = pieces * strip
    lat_width = GROUPS * LATENT
    my_z, my_core, my_dp = lax.axis_index("z"), lax.axis_index("core"), lax.axis_index(DP)
    shard = norm1_gain.shape[0]
    slice_ff = w_down.shape[0]
    wide_ff = -(-slice_ff // 128) * 128
    half = shard // 2

    gains = jnp.pad(jnp.concatenate([norm1_gain, norm2_gain])[None, :], ((0, 15), (0, lat_width - 2 * shard)))
    own_head = jnp.concatenate([my_half(w_latent), gains], axis=0)
    place = jnp.stack([my_core, my_dp, my_z]).astype(jnp.int32)
    by_step = gather_dp(own_head)
    pack = lax.all_gather(
        jnp.concatenate([my_half(w_query), my_half(w_key_up), my_half(w_value_up), my_half(w_out)], axis=0),
        CHIP,
        axis=0,
    )

    table, tables = positions_of(place, seq_lengths, pieces, nz, strip)

    tok_rows = tokens[0].reshape(rows, width)
    normed, latent, gains, latent_w = front(place, tok_rows, by_step, swap_core(jnp.stack(by_step)))
    latent = latent.reshape(pieces, strip, lat_width)
    gain_one, gain_two = gains[0:1], gains[8:9]
    tok = tok_rows.astype(F32)
    inv_one = inverse_rms(tok)
    behind = [from_behind(latent, step) for step in range(1, nz)]
    pack, cut_ff, *behind = together(pack, cut_columns(place, w_gate, w_up, ndp, half), *behind)
    sliced = lax.all_to_all(cut_ff, DP, 0, 0, tiled=True)
    up_half = w_key_up.shape[0] // 2
    cuts = [0, half, half + up_half, half + 2 * up_half, 2 * half + 2 * up_half]
    pack, grad_in = together(pack, out_grad[0].reshape(rows, width))
    query_w, key_w, value_w, out_w = (pack[:, a:b].reshape(-1, width) for a, b in zip(cuts[:-1], cuts[1:]))
    queries = mm(normed, query_w).astype(BF16)
    core_lat = [latent, *behind]
    latents = core_lat + [swap_core(x) for x in core_lat]

    grad_rows = out_grad[0].reshape(rows, width)
    grad_blocks = lax.all_gather(grad_in, DP, axis=0)
    cut = pieces // 2
    chunks = [(cut, pieces - cut), (0, cut)]

    def rows_of(x, chunk):
        return x[chunk[0] * strip : (chunk[0] + chunk[1]) * strip]

    def pieces_of(x, chunk):
        return x[chunk[0] : chunk[0] + chunk[1]]

    kept = []
    for chunk in chunks:
        absorbed, mixed, lse, heads_out = attention_forward(
            *chunk, tables, pieces_of(table, chunk), latents, rows_of(queries, chunk), key_w, value_w,
            [kept[0][6][0], sliced] if kept else [],
        )
        if kept:
            heads_out, *fresh = together(heads_out, *kept[0][6])
            kept[0][6][:] = fresh
        resid = rows_of(tok, chunk) + mm(heads_out, out_w)
        inv_two = inverse_rms(resid)
        normed_two = (resid * inv_two * gain_two).astype(BF16)
        kept.append((absorbed, mixed, lse, heads_out, resid, inv_two, gather_dp(normed_two)))

    normed_in, kept[1][6][0] = together(normed, kept[1][6][0])
    normed_stream = lax.all_gather(normed_in.reshape(pieces, strip, width), SEQ, axis=0)

    sliced_other = swap_core(sliced)
    ff_sides = []
    ff_parts = []
    for chunk, state in zip(chunks, kept):
        blocks = state[6]
        out = feed_forward(
            place, chunk[0] * strip, blocks, grad_blocks, sliced, sliced_other, w_down,
            [ff_parts[0][0]] if ff_parts else [kept[1][6][0]],
        )
        ff_sides.append((blocks, out[:3]))
        ff_parts.append(out[3:])
    received = [[partner(x, step) for step, x in enumerate(parts) if step] for parts in ff_parts]
    d_resids = []
    for chunk, state, parts, others in zip(chunks, kept, ff_parts, received):
        resid, inv_two = state[4:6]
        d_normed_two = sum((x.astype(F32) for x in others), parts[0].astype(F32))
        d_resids.append(
            rows_of(grad_rows, chunk).astype(F32) + norm_pull(resid, inv_two, gain_two, d_normed_two)
        )

    down_rows = -(-slice_ff // (16 * nseq)) * 16
    own_rows = -(-shard // (16 * nseq)) * 16
    ff_pack = ff_gradients(
        place,
        [(chunk[0] * strip, chunk[1] * strip) for chunk in chunks],
        [x for blocks, _ in ff_sides for x in blocks],
        [x for _, sides in ff_sides for x in sides],
        grad_blocks,
        nseq,
        (down_rows, own_rows),
        [],
    )
    down_wide = jnp.pad(w_down, ((0, wide_ff - slice_ff), (0, 0)))
    ff_whole = ff_pack

    ff_pack = lax.psum_scatter(ff_pack, SEQ, scatter_dimension=0, tiled=True)[0]

    order_of = [chunks.index((0, cut)), chunks.index((cut, pieces - cut))]
    d_resid = jnp.concatenate([d_resids[i] for i in order_of])
    resid = jnp.concatenate([kept[i][4] for i in order_of])
    heads_out = jnp.concatenate([kept[i][3] for i in order_of])
    d_resid_round = d_resid.astype(BF16)
    d_heads = mm_nt(d_resid_round, out_w).astype(BF16)
    absorbed, mixed, lse = ([kept[i][which] for i in order_of] for which in range(3))
    d_queries, d_lat, part_mine, part_theirs = attention_backward(
        tables, place, latents, table, queries, key_w, value_w, normed, heads_out, d_resid_round, normed_stream,
        absorbed, mixed, lse, d_heads, ndp, [ff_whole],
    )
    ff_pack, part_theirs = together(ff_pack, part_theirs)
    part_other = swap_core(part_theirs)
    chip_parts = [
        (part_mine[i].astype(F32) + part_other[i].astype(F32)).astype(BF16) for i in range(ndp)
    ]
    d_lat, *chip_parts = together(d_lat, *chip_parts)
    out_sides = together(chip_parts[0], *[sides[0] for _, sides in ff_sides])
    chip_parts[0] = out_sides[0]
    out_parts = [mm(x, down_wide).astype(BF16) for x in out_sides[1:]]
    core_sum = d_lat[:nz].astype(F32) + swap_core(d_lat[nz:]).astype(F32)
    send = core_sum.astype(BF16)
    d_latent = core_sum[0]
    for step in range(1, nz):
        d_latent = d_latent + from_ahead(send[step], step).astype(F32)
    d_latent = d_latent.astype(BF16).reshape(rows, lat_width)
    down_lines = down_rows * width // 128
    swap = ff_pack[down_lines:].reshape(ndp, -1, 128)
    swap = lax.all_to_all(swap, DP, 0, 0, tiled=True)
    ff_pack = jnp.concatenate([ff_pack[:down_lines], swap.reshape(-1, 128)], axis=0)
    ff_gathered = lax.all_gather(ff_pack, SEQ, axis=0)
    d_normed = mm_nt(d_queries, query_w) + mm_nt(d_latent, latent_w)
    tokens_grad = (d_resid + norm_pull(tok, inv_one, gain_one, d_normed)).astype(BF16)
    block = []
    for i in range(ndp):
        parts = [x[i * chunk[1] * strip : (i + 1) * chunk[1] * strip] for x, chunk in zip(out_parts, chunks)]
        block.append(jnp.concatenate([parts[j] for j in order_of]))
    layer_out = (resid + scatter_dp(block)).astype(BF16)

    grad_pack = scatter_dp(chip_parts).astype(BF16)
    own, ff_gathered = together(grad_pack, ff_gathered)
    own = own.reshape(nz, -1, width)
    down_out, gate_out, up_out, gain_two_sum = unpack_ff(
        ff_gathered, w_gate, w_up, slice_ff, width, own_rows, down_rows
    )
    own = lax.psum_scatter(own, "z", scatter_dimension=0, tiled=True)
    own, gain_two_sum = together(own[0], gain_two_sum)
    own = lax.all_gather(own, SEQ, axis=0).reshape(nz, 2, -1, width)
    lat_rows = half * lat_width // width
    sections = (half, up_half, up_half, half, lat_rows)
    if own.shape[2] % 32 == 0:
        query_out, key_out, value_out, out_out, latent_out, gain_one_sum = unpack_attention(
            own, w_query, w_latent, sections
        )
    else:
        own = own.transpose(1, 0, 2, 3).reshape(2, -1, width).astype(F32)
        query_out, key_out, value_out, out_out, latent_out = (
            own[:, cut : cut + count].reshape(-1, width) for cut, count in zip([*cuts[:-1], cuts[-1]], sections)
        )
        fold = width // lat_width
        latent_out = latent_out.reshape(2, lat_rows, fold, lat_width).transpose(0, 2, 1, 3).reshape(shard, lat_width)
        gain_one_sum = jnp.sum(w_query.astype(F32) * query_out, axis=1, keepdims=True)
        gain_one_sum += jnp.sum(w_latent.astype(F32) * latent_out, axis=1, keepdims=True)

    gain_one_out = gain_one_sum[:, 0] / norm1_gain.astype(F32)
    gain_two_out = gain_two_sum[:, 0] / norm2_gain.astype(F32)

    shape = (1, pieces, strip, width)
    return (
        layer_out.reshape(shape), tokens_grad.reshape(shape), gain_one_out, query_out, latent_out, key_out,
        value_out, out_out, gain_two_out, gate_out, up_out, down_out,
    )


def solution(mesh):
    sizes = mesh.shape
    grid = Mesh(mesh.devices.reshape(sizes["dp"], sizes["seq"] // 2, 2), ("dp", "z", "core"))
    stream = P("dp", None, SEQ, None)
    vector, matrix = P("dp"), P("dp", None)
    in_specs = (
        stream, vector, matrix, matrix, matrix, matrix, matrix, vector, matrix, matrix, matrix, stream, matrix,
    )
    out_specs = (
        stream, stream, vector, matrix, matrix, matrix, matrix, matrix, vector, matrix, matrix, matrix,
    )
    return jax.shard_map(per_device, mesh=grid, in_specs=in_specs, out_specs=out_specs, check_vma=False)
```

```python
import functools
import math

import jax
import jax.numpy as jnp
from jax import lax
from jax.experimental import pallas as pl
from jax.experimental.pallas import tpu as pltpu
from jax.sharding import Mesh
from jax.sharding import PartitionSpec as P

HEADS = 16
HEAD_DIM = 64
GROUPS = 2
LATENT = 256
PER_GROUP = HEADS // GROUPS
GROUP_COLS = PER_GROUP * HEAD_DIM
KEY_BLOCK = 256
VMEM_FORWARD = 56
VMEM_BACKWARD = 56
SCALE = 1.0 / math.sqrt(HEAD_DIM)
NEG_FILL = -1e30
NORM_EPS = 1e-05
F32 = jnp.float32
BF16 = jnp.bfloat16
DP = "dp"
SEQ = ("z", "core")
NO_COST = pl.CostEstimate(flops=0, transcendentals=0, bytes_accessed=0)
CHIP = ("dp", "core")


def mm(a, b):
    return jnp.dot(a, b, preferred_element_type=F32)


def mm_nt(a, b):
    return lax.dot_general(a, b, (((1,), (1,)), ((), ())), preferred_element_type=F32)


def mm_tn(a, b):
    return lax.dot_general(a, b, (((0,), (0,)), ((), ())), preferred_element_type=F32)


def low_lanes(rows):
    return lax.broadcasted_iota(jnp.int32, (rows, 2 * HEAD_DIM), 1) < HEAD_DIM


def pair_cols(pair):
    return slice(2 * HEAD_DIM * pair, 2 * HEAD_DIM * (pair + 1))


def expand_pair(part, proj):
    low = low_lanes(part.shape[0])
    zero = jnp.zeros_like(part)
    both = jnp.concatenate([jnp.where(low, part, zero), jnp.where(low, zero, part)], axis=0)
    return mm_nt(both, proj)


def shrink_pair(parts, proj):
    rows = parts.shape[0] // 2
    both = mm(parts, proj)
    return jnp.where(low_lanes(rows), both[:rows], both[rows:])


def outer_pair(parts, vals):
    rows = vals.shape[0]
    return jnp.where(low_lanes(LATENT), mm_tn(parts[:rows], vals), mm_tn(parts[rows:], vals))


def load_keys(lat_ref, slot_ref, block, strips, per_piece):
    piece = block // per_piece
    first = (block - piece * per_piece) * strips
    parts = [lat_ref[slot_ref[first + i], piece] for i in range(strips)]
    return jnp.concatenate(parts, axis=0), piece, first


def visible(block, base, starts, rows):
    key_pos = block * KEY_BLOCK + lax.broadcasted_iota(jnp.int32, (KEY_BLOCK, 2 * rows), 0)
    row_pos = base + lax.broadcasted_iota(jnp.int32, (KEY_BLOCK, 2 * rows), 1) % rows
    return (key_pos >= starts) & (key_pos <= row_pos)


def masked(scores, seen):
    wide = seen.shape[1]
    parts = [
        jnp.where(seen, scores[:, i * wide : (i + 1) * wide], NEG_FILL) for i in range(scores.shape[1] // wide)
    ]
    return jnp.concatenate(parts, axis=1)


def copies(sources, target_ref, sem):
    return [
        pltpu.make_async_copy(source, target_ref.at[slot], sem.at[slot]) for slot, source in enumerate(sources)
    ]


def latent_cols(group):
    return slice(group * LATENT, (group + 1) * LATENT)


def forward_body(first_piece, nseq, waits, lo_ref, hi_ref, base_ref, slot_ref, *refs):
    sources, refs = refs[:nseq], refs[nseq + waits :]
    start_ref, query_ref, key_up_ref, value_up_ref = refs[:4]
    abs_ref, mixed_ref, lse_ref, out_ref, top_ref, sum_ref, acc_ref, lat_ref, lat_sem = refs[4:]
    fetches = copies(sources, lat_ref, lat_sem)
    for fetch in fetches:
        fetch.start()
    strip = lat_ref.shape[2]
    groups, _, count = mixed_ref.shape[:3]
    strips = KEY_BLOCK // strip
    per_piece = nseq // strips
    tall = PER_GROUP * strip
    pairs = PER_GROUP // 2
    for pair in range(groups * pairs):
        cols = pair_cols(pair)
        part = expand_pair(query_ref[:, cols], key_up_ref[:, cols])
        part = part.astype(BF16) * jnp.asarray(SCALE, BF16)
        first = 2 * (pair % pairs)
        abs_ref[pair // pairs, first : first + 2] = part.reshape(2, count, strip, LATENT)
    for fetch in fetches:
        fetch.wait()

    for index in range(count):
        piece_id = index + first_piece
        top_ref[...] = jnp.full(top_ref.shape, NEG_FILL, F32)
        sum_ref[...] = jnp.zeros(sum_ref.shape, F32)
        acc_ref[...] = jnp.zeros(acc_ref.shape, F32)
        starts = jnp.broadcast_to(start_ref[index, 0:1], (KEY_BLOCK, 2 * strip))

        def step(block, carry):
            keys, _, _ = load_keys(lat_ref, slot_ref, block, strips, per_piece)
            keys = [keys[:, latent_cols(g)] for g in range(groups)]
            seen = visible(block, base_ref[piece_id], starts, strip)
            tops = [top_ref[g] for g in range(groups)]
            sums = [sum_ref[g] for g in range(groups)]
            raw = [mm_nt(keys[g], abs_ref[g, :, index].reshape(tall, LATENT)) for g in range(groups)]
            done = []
            for g in range(groups):
                scores = masked(raw[g], seen)
                new_top = jnp.maximum(tops[g], jnp.max(scores, axis=0, keepdims=True))
                shrink = jnp.exp(tops[g] - new_top)
                probs = jnp.exp(scores - new_top)
                total = sums[g] * shrink + jnp.sum(probs, axis=0, keepdims=True)
                done.append((new_top, total, shrink, mm_tn(keys[g], probs.astype(BF16))))
            for g in range(groups):
                new_top, total, shrink, term = done[g]
                top_ref[g] = new_top
                sum_ref[g] = total
                acc_ref[g] = acc_ref[g] * shrink + term
            return carry

        lax.fori_loop(lo_ref[piece_id], hi_ref[piece_id], step, 0)
        for g in range(groups):
            total = sum_ref[g]
            lse_ref[g, index] = jnp.broadcast_to(top_ref[g] + jnp.log(total), (8, tall))
            mixed = (acc_ref[g] * (1.0 / total)).T.astype(BF16)
            mixed_ref[g, :, index] = mixed.reshape(PER_GROUP, strip, LATENT)

    for pair in range(groups * pairs):
        cols = pair_cols(pair)
        first = 2 * (pair % pairs)
        parts = mixed_ref[pair // pairs, first : first + 2].reshape(2 * count * strip, LATENT)
        out_ref[:, cols] = shrink_pair(parts, value_up_ref[:, cols]).astype(BF16)


def backward_body(nseq, waits, lo_ref, hi_ref, base_ref, slot_ref, place_ref, *refs):
    sources, refs = refs[:nseq], refs[nseq + waits :]
    start_ref, query_ref, key_up_ref, value_up_ref, normed_ref, out_ref, resid_grad_ref, normed_hbm = refs[:8]
    abs_front, abs_back, mixed_front, mixed_back, lse_front, lse_back, grad_ref = refs[8:15]
    dquery_ref, dlat_hbm, mine_ref, theirs_ref = refs[15:19]
    dmix_ref, delta_ref, acc_ref, dabs_ref, dkey_ref, latent_sum_ref, stage_ref, lat_ref, lat_sem = refs[19:28]
    stream_ref, stream_sem, dlat_sem = refs[28:]
    fetches = copies(sources, lat_ref, lat_sem)
    for fetch in fetches:
        fetch.start()
    _, pieces, strip, _ = lat_ref.shape
    groups, _, cut = mixed_front.shape[:3]
    strips = KEY_BLOCK // strip
    per_piece = nseq // strips
    tall = PER_GROUP * strip
    pairs = PER_GROUP // 2
    depth = stream_ref.shape[0]
    my_core, my_dp = place_ref[0], place_ref[1]
    ndp = mine_ref.shape[0]

    def fetch_stream(seq):
        slot = seq % depth
        return pltpu.make_async_copy(normed_hbm.at[seq], stream_ref.at[slot], stream_sem.at[slot])

    for seq in range(depth):
        fetch_stream(seq).start()

    def give(first, grad):
        rows = grad.shape[0] // (2 * ndp)
        for dp in range(ndp):
            for core in range(2):
                part = grad[(2 * dp + core) * rows : (2 * dp + core + 1) * rows]

                @pl.when(my_core == core)
                def _():
                    mine_ref[dp ^ my_dp, first : first + rows] = part

                @pl.when(my_core != core)
                def _():
                    theirs_ref[dp ^ my_dp, first : first + rows] = part

    def of_pair(g, first):
        parts = [ref[g, first : first + 2] for ref in (mixed_front, mixed_back)]
        return jnp.concatenate(parts, axis=1).reshape(2 * pieces * strip, LATENT)

    def clear(slot, carry):
        dkey_ref[slot] = jnp.zeros(dkey_ref.shape[1:], F32)
        return carry

    lax.fori_loop(0, nseq, clear, 0)
    for pair in range(groups * pairs):
        cols = pair_cols(pair)
        g, first = pair // pairs, 2 * (pair % pairs)
        grads = grad_ref[:, cols]
        part = expand_pair(grads, value_up_ref[:, cols]).astype(BF16)
        dmix_ref[g, first : first + 2] = part.reshape(2, pieces, strip, LATENT)
        stage_ref[0, :, cols] = outer_pair(of_pair(g, first), grads).astype(BF16)
    for fetch in fetches:
        fetch.wait()

    for piece_id in range(pieces):
        index = piece_id if piece_id < cut else piece_id - cut
        front = piece_id < cut
        abs_ref, mixed_ref, lse_ref = (
            (abs_front, mixed_front, lse_front) if front else (abs_back, mixed_back, lse_back)
        )
        for g in range(groups):
            dmix_all = dmix_ref[g, :, piece_id].reshape(tall, LATENT).astype(F32)
            mixed_all = mixed_ref[g, :, index].reshape(tall, LATENT).astype(F32)
            delta = jnp.sum(dmix_all * mixed_all, axis=1, keepdims=True)
            delta_ref[g] = jnp.broadcast_to(delta, (tall, 128)).T[:8]
        acc_ref[...] = jnp.zeros(acc_ref.shape, F32)
        starts = jnp.broadcast_to(start_ref[piece_id, 0:1], (KEY_BLOCK, 2 * strip))

        def step(block, carry):
            keys, key_piece, first = load_keys(lat_ref, slot_ref, block, strips, per_piece)
            keys = [keys[:, latent_cols(g)] for g in range(groups)]
            seen = visible(block, base_ref[piece_id], starts, strip)
            absorbed = [abs_ref[g, :, index].reshape(tall, LATENT) for g in range(groups)]
            dmix = [dmix_ref[g, :, piece_id].reshape(tall, LATENT) for g in range(groups)]
            raw = [(mm_nt(keys[g], absorbed[g]), mm_nt(keys[g], dmix[g])) for g in range(groups)]
            done = []
            for g in range(groups):
                probs = jnp.exp(masked(raw[g][0] - lse_ref[g, index, 0:1], seen))
                d_scores = (probs * (raw[g][1] - delta_ref[g, 0:1])).astype(BF16)
                d_keys = mm(d_scores, absorbed[g]) + mm(probs.astype(BF16), dmix[g])
                done.append((mm_tn(d_scores, keys[g]), d_keys))
            for g in range(groups):
                acc_ref[g] += done[g][0]
                for i in range(strips):
                    part = done[g][1][i * strip : (i + 1) * strip]
                    dkey_ref[slot_ref[first + i], key_piece, :, latent_cols(g)] += part
            return carry

        lax.fori_loop(lo_ref[piece_id], hi_ref[piece_id], step, 0)
        for g in range(groups):
            dabs_ref[g, :, piece_id] = (acc_ref[g] * SCALE).astype(BF16).reshape(PER_GROUP, strip, LATENT)

    def settle(slot, carry):
        lat_ref[slot] = dkey_ref[slot].astype(BF16)
        return carry

    lax.fori_loop(0, nseq, settle, 0)
    send = pltpu.make_async_copy(lat_ref, dlat_hbm, dlat_sem)
    send.start()
    for pair in range(groups * pairs):
        cols = pair_cols(pair)
        g, first = pair // pairs, 2 * (pair % pairs)
        parts = dabs_ref[g, first : first + 2].reshape(2 * pieces * strip, LATENT)
        dquery_ref[:, cols] = shrink_pair(parts, key_up_ref[:, cols]).astype(BF16)
        stage_ref[1, :, cols] = outer_pair(parts, query_ref[:, cols]).astype(BF16)

    width = normed_ref.shape[1]
    half = width // (2 * ndp)
    up_half = LATENT // (2 * ndp)
    give(0, mm_tn(normed_ref[...], dquery_ref[...]).astype(BF16))
    give(half, stage_ref[1])
    give(half + up_half, stage_ref[0])
    give(half + 2 * up_half, mm_tn(out_ref[...], resid_grad_ref[...]).astype(BF16))
    latent_sum_ref[...] = jnp.zeros(latent_sum_ref.shape, F32)

    def latent_term(seq, carry):
        fetch_stream(seq).wait()
        rows = stream_ref[seq % depth].reshape(pieces * strip, width)
        grads = lat_ref[slot_ref[seq]].reshape(pieces * strip, groups * LATENT)
        latent_sum_ref[...] += mm_tn(rows, grads)

        @pl.when(seq + depth < nseq)
        def _():
            fetch_stream(seq + depth).start()

        return carry

    lax.fori_loop(0, nseq, latent_term, 0)
    lat_width = groups * LATENT
    fold = width // lat_width
    latent_grad = latent_sum_ref[...].astype(BF16).reshape(2 * ndp, fold, half // fold, lat_width)
    latent_grad = [latent_grad[:, i].reshape(width // fold, lat_width) for i in range(fold)]
    give(2 * half + 2 * up_half, jnp.concatenate(latent_grad, axis=1))
    send.wait()


def attention_specs(strip, pieces):
    tall = PER_GROUP * strip

    def whole(*shape):
        return pl.BlockSpec(shape, lambda *_: (0,) * len(shape), pipeline_mode=pl.Buffered(1))

    table = whole(pieces, 8, 2 * strip)
    rows = whole(pieces * strip, GROUPS * GROUP_COLS)
    proj = whole(LATENT, GROUPS * GROUP_COLS)
    heads = whole(GROUPS, PER_GROUP, pieces, strip, LATENT)
    lse = whole(GROUPS, pieces, 8, tall)
    return whole, table, rows, proj, heads, lse


def kernel_params(vmem):
    return pltpu.CompilerParams(dimension_semantics=("arbitrary",), vmem_limit_bytes=vmem << 20)


def attention_forward(first_piece, pieces, tables, table, latents, queries, key_up, value_up, waits):
    nseq = len(latents)
    strip = latents[0].shape[1]
    tall = PER_GROUP * strip
    _, t_spec, row_spec, proj_spec, head_spec, lse_spec = attention_specs(strip, pieces)
    head_shape = jax.ShapeDtypeStruct((GROUPS, PER_GROUP, pieces, strip, LATENT), BF16)
    in_place = pl.BlockSpec(memory_space=pl.ANY)
    return pl.pallas_call(
        functools.partial(forward_body, first_piece, nseq, len(waits)),
        name="attention_forward",
        grid_spec=pltpu.PrefetchScalarGridSpec(
            num_scalar_prefetch=len(tables),
            grid=(1,),
            in_specs=[in_place] * (nseq + len(waits)) + [t_spec, row_spec, proj_spec, proj_spec],
            out_specs=[head_spec, head_spec, lse_spec, row_spec],
            scratch_shapes=[
                pltpu.VMEM((GROUPS, 1, tall), F32),
                pltpu.VMEM((GROUPS, 1, tall), F32),
                pltpu.VMEM((GROUPS, LATENT, tall), F32),
                pltpu.VMEM((nseq, *latents[0].shape), BF16),
                pltpu.SemaphoreType.DMA((nseq,)),
            ],
        ),
        out_shape=[
            head_shape,
            head_shape,
            jax.ShapeDtypeStruct((GROUPS, pieces, 8, tall), F32),
            jax.ShapeDtypeStruct((pieces * strip, queries.shape[1]), BF16),
        ],
        compiler_params=kernel_params(VMEM_FORWARD if nseq <= 8 else 56),
        cost_estimate=NO_COST,
    )(*tables, *latents, *waits, table, queries, key_up, value_up)


def attention_backward(
    tables, place, latents, table, queries, key_up, value_up, normed, heads_out, resid_grads, normed_stream,
    absorbed, mixed, lse, grads, ndp, waits,
):
    nseq = len(latents)
    pieces, strip, lat_width = latents[0].shape
    tall = PER_GROUP * strip
    cut = mixed[0].shape[2]
    whole, t_spec, row_spec, proj_spec, _, _ = attention_specs(strip, pieces)
    head_front, lse_front = attention_specs(strip, cut)[4:]
    head_back, lse_back = attention_specs(strip, pieces - cut)[4:]
    width = normed_stream.shape[3]
    depth = nseq if nseq <= 8 else 2
    part = (ndp, (2 * width + 2 * LATENT + lat_width * width // key_up.shape[1]) // (2 * ndp), width)
    in_place = pl.BlockSpec(memory_space=pl.ANY)
    return pl.pallas_call(
        functools.partial(backward_body, nseq, len(waits)),
        name="attention_backward",
        grid_spec=pltpu.PrefetchScalarGridSpec(
            num_scalar_prefetch=len(tables) + 1,
            grid=(1,),
            in_specs=[in_place] * (nseq + len(waits)) + [
                t_spec, row_spec, proj_spec, proj_spec, row_spec, row_spec, row_spec, in_place,
                head_front, head_back, head_front, head_back, lse_front, lse_back, row_spec,
            ],
            out_specs=[row_spec, in_place, whole(*part), whole(*part)],
            scratch_shapes=[
                pltpu.VMEM((GROUPS, PER_GROUP, pieces, strip, LATENT), BF16),
                pltpu.VMEM((GROUPS, 8, tall), F32),
                pltpu.VMEM((GROUPS, tall, LATENT), F32),
                pltpu.VMEM((GROUPS, PER_GROUP, pieces, strip, LATENT), BF16),
                pltpu.VMEM((nseq, pieces, strip, lat_width), F32),
                pltpu.VMEM((width, lat_width), F32),
                pltpu.VMEM((2, LATENT, GROUPS * GROUP_COLS), BF16),
                pltpu.VMEM((nseq, pieces, strip, lat_width), BF16),
                pltpu.SemaphoreType.DMA((nseq,)),
                pltpu.VMEM((depth, *normed_stream.shape[1:]), BF16),
                pltpu.SemaphoreType.DMA((depth,)),
                pltpu.SemaphoreType.DMA,
            ],
        ),
        out_shape=[
            jax.ShapeDtypeStruct(queries.shape, BF16),
            jax.ShapeDtypeStruct((nseq, pieces, strip, lat_width), BF16),
            jax.ShapeDtypeStruct(part, BF16),
            jax.ShapeDtypeStruct(part, BF16),
        ],
        compiler_params=kernel_params(VMEM_BACKWARD if nseq <= 8 else 62),
        cost_estimate=NO_COST,
    )(
        *tables, place, *latents, *waits, table, queries, key_up, value_up, normed, heads_out, resid_grads, normed_stream,
        *absorbed, *mixed, *lse, grads,
    )


def positions_body(pieces, nz, strip, place_ref, lengths_ref, table_ref, lo_ref, hi_ref, base_ref, slot_ref):
    my_core, my_z = place_ref[0], place_ref[2]
    span = strip * 2 * nz
    mine = (2 * my_z + my_core) * strip
    wide = table_ref.shape[2]
    lane = lax.broadcasted_iota(jnp.int32, (1, wide), 1) % strip
    positions = [piece * span + mine + lane for piece in range(pieces)]
    ids = [piece * span + mine for piece in range(pieces)]

    def entry(i, carry):
        first, starts, lows = carry
        end = first + lengths_ref[0, 2 * i]
        starts = [jnp.where((p >= first) & (p < end), first, s) for p, s in zip(positions, starts)]
        lows = [jnp.where((p >= first) & (p < end), first, s) for p, s in zip(ids, lows)]
        return end + lengths_ref[0, 2 * i + 1], starts, lows

    _, starts, lows = lax.fori_loop(0, lengths_ref.shape[1] // 2, entry, (jnp.int32(0), positions, ids))
    for piece in range(pieces):
        table_ref[piece] = jnp.broadcast_to(starts[piece], table_ref.shape[1:])
        lo_ref[piece] = lows[piece] // KEY_BLOCK
        hi_ref[piece] = (ids[piece] + strip + KEY_BLOCK - 1) // KEY_BLOCK
        base_ref[piece] = ids[piece]
    for seq in range(2 * nz):
        core = jnp.where(my_core == seq % 2, 0, 1)
        slot_ref[seq] = core * nz + jnp.where(my_z >= seq // 2, my_z - seq // 2, my_z - seq // 2 + nz)


def positions_of(place, lengths, pieces, nz, strip):
    small = pl.BlockSpec(memory_space=pltpu.SMEM)
    counts = [pieces, pieces, pieces, 2 * nz]
    table, *tables = pl.pallas_call(
        functools.partial(positions_body, pieces, nz, strip),
        name="positions",
        grid_spec=pltpu.PrefetchScalarGridSpec(
            num_scalar_prefetch=1,
            grid=(1,),
            in_specs=[small],
            out_specs=[whole_spec(pieces, 8, 2 * strip)] + [small] * 4,
        ),
        out_shape=[jax.ShapeDtypeStruct((pieces, 8, 2 * strip), jnp.int32)]
        + [jax.ShapeDtypeStruct((count,), jnp.int32) for count in counts],
        cost_estimate=NO_COST,
    )(place, lengths)
    return table, tuple(tables)


def cut_body(place_ref, gate_hbm, up_hbm, out_ref, rows_ref, sems):
    ndp, _, half, wide = out_ref.shape
    first = pl.multiple_of(place_ref[0] * half, half)
    fetches = [
        pltpu.make_async_copy(source.at[pl.ds(first, half)], rows_ref.at[i], sems.at[i])
        for i, source in enumerate((gate_hbm, up_hbm))
    ]
    for fetch in fetches:
        fetch.start()
    slice_ff = gate_hbm.shape[1] // ndp
    low = lax.broadcasted_iota(jnp.int32, (half, 128), 1) < 64
    zero = jnp.zeros((half, 128), F32)
    whole_tiles = slice_ff // 128
    for which, fetch in enumerate(fetches):
        fetch.wait()

        def tile_of(t):
            return rows_ref[which, :, t * 128 : (t + 1) * 128].astype(F32)

        for dp in range(ndp):
            first_tile = dp * slice_ff // 128
            if dp % 2 == 0:
                parts = [tile_of(first_tile + t) for t in range(whole_tiles)]
                parts.append(jnp.where(low, tile_of(first_tile + whole_tiles), zero))
            else:
                halves = [pltpu.roll(tile_of(first_tile + t), 64, 1) for t in range(whole_tiles + 1)]
                parts = [jnp.where(low, halves[t], halves[t + 1]) for t in range(whole_tiles)]
                parts.append(jnp.where(low, halves[whole_tiles], zero))
            for t, part in enumerate(parts):
                out_ref[dp, which, :, t * 128 : (t + 1) * 128] = part.astype(BF16)


def cut_columns(place, w_gate, w_up, ndp, half):
    ff = w_gate.shape[1]
    wide = -(-ff // ndp // 128) * 128
    in_place = pl.BlockSpec(memory_space=pl.ANY)
    return pl.pallas_call(
        cut_body,
        name="cut_columns",
        grid_spec=pltpu.PrefetchScalarGridSpec(
            num_scalar_prefetch=1,
            grid=(1,),
            in_specs=[in_place, in_place],
            out_specs=whole_spec(ndp, 2, half, wide),
            scratch_shapes=[pltpu.VMEM((2, half, ff), BF16), pltpu.SemaphoreType.DMA((2,))],
        ),
        out_shape=jax.ShapeDtypeStruct((ndp, 2, half, wide), BF16),
        compiler_params=kernel_params(16),
        cost_estimate=NO_COST,
    )(place, w_gate, w_up)


def front_body(ndp, place_ref, tok_ref, *refs):
    blocks, refs = refs[:ndp], refs[ndp:]
    other_hbm, normed_ref, latent_ref, gain_out_ref, weight_ref, gain_ref, sems = refs
    my_core, my_dp = place_ref[0], place_ref[1]
    half = other_hbm.shape[1] - 16
    width = tok_ref.shape[1]
    shard = 2 * half
    fetches = []
    for i in range(ndp):
        dp = my_dp ^ i
        for core, source in enumerate((blocks[i], other_hbm.at[i])):
            first = pl.multiple_of(dp * shard + (my_core ^ core) * half, half)
            fetches.append((source.at[pl.ds(0, half)], weight_ref.at[pl.ds(first, half)]))
        fetches.append((blocks[i].at[pl.ds(half, 16)], gain_ref.at[dp]))
    fetches = [pltpu.make_async_copy(a, b, sems.at[i]) for i, (a, b) in enumerate(fetches)]
    for fetch in fetches:
        fetch.start()
    tok = tok_ref[...].astype(F32)
    scaled = tok * inverse_rms(tok)
    for fetch in fetches:
        fetch.wait()
    gains = [gain_ref[dp].astype(F32) for dp in range(ndp)]
    gain_one = jnp.concatenate([g[0:1, :shard] for g in gains], axis=1)
    gain_two = jnp.concatenate([g[0:1, shard : 2 * shard] for g in gains], axis=1)
    normed = (scaled * gain_one).astype(BF16)
    normed_ref[...] = normed
    latent_ref[...] = mm(normed, weight_ref[...]).astype(BF16)
    gain_out_ref[0:8] = jnp.broadcast_to(gain_one, (8, width))
    gain_out_ref[8:16] = jnp.broadcast_to(gain_two, (8, width))


def front(place, tok, blocks, other):
    rows, width = tok.shape
    ndp = len(blocks)
    lat_width = other.shape[2]
    in_place = pl.BlockSpec(memory_space=pl.ANY)
    return pl.pallas_call(
        functools.partial(front_body, ndp),
        name="front",
        grid_spec=pltpu.PrefetchScalarGridSpec(
            num_scalar_prefetch=1,
            grid=(1,),
            in_specs=[whole_spec(rows, width)] + [in_place] * (ndp + 1),
            out_specs=[
                whole_spec(rows, width), whole_spec(rows, lat_width), whole_spec(16, width),
                whole_spec(width, lat_width),
            ],
            scratch_shapes=[
                pltpu.VMEM((ndp, 16, lat_width), BF16),
                pltpu.SemaphoreType.DMA((3 * ndp,)),
            ],
        ),
        out_shape=[
            jax.ShapeDtypeStruct((rows, width), BF16),
            jax.ShapeDtypeStruct((rows, lat_width), BF16),
            jax.ShapeDtypeStruct((16, width), F32),
            jax.ShapeDtypeStruct((width, lat_width), BF16),
        ],
        compiler_params=kernel_params(16),
        cost_estimate=NO_COST,
    )(place, tok, *blocks, other)


def ff_body(ndp, first_row, waits, place_ref, *refs):
    blocks, refs = refs[:ndp], refs[ndp + waits :]
    grad_hbm, mine_hbm, theirs_hbm, down_hbm = refs[:4]
    hidden_ref, dgate_ref, dup_ref = refs[4:7]
    part_refs, refs = refs[7 : 7 + ndp], refs[7 + ndp :]
    weight_ref, down_ref, grad_ref, weight_sem, down_sem, grad_sem = refs
    my_core, my_dp = place_ref[0], place_ref[1]
    size, width = blocks[0].shape
    slice_ff = down_hbm.shape[0]
    wide = hidden_ref.shape[1]
    half = mine_hbm.shape[2]
    fetch_down = pltpu.make_async_copy(down_hbm, down_ref.at[pl.ds(0, slice_ff)], down_sem)
    fetch_down.start()
    fetch_grads = [
        pltpu.make_async_copy(
            grad_hbm.at[2 * (my_dp ^ i) + my_core, pl.ds(first_row, size)],
            grad_ref.at[pl.ds(i * size, size)],
            grad_sem.at[i],
        )
        for i in range(ndp)
    ]
    for fetch in fetch_grads:
        fetch.start()
    fetch_weights = []
    for which in range(2):
        for dp in range(ndp):
            for core, source in enumerate((mine_hbm, theirs_hbm)):
                first = pl.multiple_of((2 * dp + (my_core ^ core)) * half, half)
                fetch_weights.append(
                    pltpu.make_async_copy(
                        source.at[dp, which], weight_ref.at[which, pl.ds(first, half)],
                        weight_sem.at[which, 2 * dp + core],
                    )
                )
    for fetch in fetch_weights:
        fetch.start()
    if wide > slice_ff:
        down_ref[slice_ff:] = jnp.zeros((wide - slice_ff, width), BF16)
    fetch_down.wait()
    for fetch in fetch_grads + fetch_weights:
        fetch.wait()
    per = max(ndp // 2, 1)
    for first in range(0, ndp, per):
        span = slice(first * size, (first + per) * size)
        normed = jnp.concatenate([blocks[i][...] for i in range(first, first + per)], axis=0)
        gate = mm(normed, weight_ref[0])
        up = mm(normed, weight_ref[1])
        d_hidden = mm_nt(grad_ref[span], down_ref[...])
        sig = 1.0 / (1.0 + jnp.exp(-gate))
        silu = gate * sig
        hidden_ref[span] = (silu * up).astype(BF16)
        d_gate = (d_hidden * up * (sig * (1.0 + gate * (1.0 - sig)))).astype(BF16)
        d_up = (d_hidden * silu).astype(BF16)
        dgate_ref[span] = d_gate
        dup_ref[span] = d_up
        part = (mm_nt(d_gate, weight_ref[0]) + mm_nt(d_up, weight_ref[1])).astype(BF16)
        for i in range(per):
            part_refs[first + i][...] = part[i * size : (i + 1) * size]


def whole_spec(*shape):
    return pl.BlockSpec(shape, lambda *_: (0,) * len(shape), pipeline_mode=pl.Buffered(1))


def feed_forward(place, first_row, blocks, grad_blocks, mine, theirs, down, waits):
    ndp = len(blocks)
    size, width = blocks[0].shape
    wide = mine.shape[3]
    in_place = pl.BlockSpec(memory_space=pl.ANY)
    tall = jax.ShapeDtypeStruct((ndp * size, wide), BF16)
    return pl.pallas_call(
        functools.partial(ff_body, ndp, first_row, len(waits)),
        name="feed_forward",
        grid_spec=pltpu.PrefetchScalarGridSpec(
            num_scalar_prefetch=1,
            grid=(1,),
            in_specs=[whole_spec(size, width)] * ndp + [in_place] * (len(waits) + 4),
            out_specs=[whole_spec(ndp * size, wide)] * 3 + [whole_spec(size, width)] * ndp,
            scratch_shapes=[
                pltpu.VMEM((2, width, wide), BF16),
                pltpu.VMEM((wide, width), BF16),
                pltpu.VMEM((ndp * size, width), BF16),
                pltpu.SemaphoreType.DMA((2, 2 * ndp)),
                pltpu.SemaphoreType.DMA,
                pltpu.SemaphoreType.DMA((ndp,)),
            ],
        ),
        out_shape=[tall] * 3 + [jax.ShapeDtypeStruct((size, width), BF16)] * ndp,
        compiler_params=kernel_params(48),
        cost_estimate=NO_COST,
    )(place, *blocks, *waits, grad_blocks, mine, theirs, down)


def ff_grad_body(ndp, nseq, spans, owned, waits, place_ref, *refs):
    blocks, refs = refs[: ndp * len(spans)], refs[ndp * len(spans) + waits :]
    sides, refs = refs[: 3 * len(spans)], refs[3 * len(spans) :]
    grad_hbm, pack_ref, normed_ref, grad_ref, hidden_ref, dgate_ref, dup_ref, sems = refs
    my_core, my_dp = place_ref[0], place_ref[1]
    width = normed_ref.shape[1]
    wide = hidden_ref.shape[1]
    down_rows, own_rows = owned
    fetches = []

    def fetch(source, target):
        copy = pltpu.make_async_copy(source, target, sems.at[len(fetches)])
        copy.start()
        fetches.append(copy)

    row = 0
    for chunk, (first_row, size) in enumerate(spans):
        for target, source in zip((hidden_ref, dgate_ref, dup_ref), sides[3 * chunk : 3 * chunk + 3]):
            fetch(source, target.at[pl.ds(row, ndp * size)])
        for i in range(ndp):
            fetch(blocks[ndp * chunk + i], normed_ref.at[pl.ds(row + i * size, size)])
            fetch(grad_hbm.at[2 * (my_dp ^ i) + my_core, pl.ds(first_row, size)], grad_ref.at[pl.ds(row + i * size, size)])
        row += ndp * size
    for copy in fetches:
        copy.wait()

    def give(seq, first, part):
        rows = part.shape[0]
        for tile in range(part.shape[1] // 128):
            pack_ref[seq, first + tile * rows : first + (tile + 1) * rows] = part[:, tile * 128 : (tile + 1) * 128]

    some = wide // 2
    for first in range(0, wide, some):
        part = mm_tn(hidden_ref[:, first : first + some], grad_ref[...]).astype(BF16)
        for i in range(some // down_rows):
            give(first // down_rows + i, 0, part[i * down_rows : (i + 1) * down_rows])
    for seq in range(wide // down_rows, nseq):
        give(seq, 0, jnp.zeros((down_rows, width), BF16))
    shard = width // ndp
    first = down_rows * width // 128
    for dp in range(ndp):
        for side in (dgate_ref, dup_ref):
            part = mm_tn(normed_ref[:, dp * shard : (dp + 1) * shard], side[...]).astype(BF16)
            for seq in range(nseq):
                if seq * own_rows < shard:
                    give(seq, first, part[seq * own_rows : (seq + 1) * own_rows])
                else:
                    give(seq, first, jnp.zeros((own_rows, wide), BF16))
            first += own_rows * wide // 128


def ff_gradients(place, spans, blocks, sides, grad_blocks, nseq, owned, waits):
    ndp = len(blocks) // len(spans)
    width = blocks[0].shape[1]
    wide = sides[0].shape[1]
    rows = ndp * sum(size for _, size in spans)
    down_rows, own_rows = owned
    pack = (nseq, (down_rows * width + 2 * ndp * own_rows * wide) // 128, 128)
    in_place = pl.BlockSpec(memory_space=pl.ANY)
    count = len(spans) * (3 + 2 * ndp)
    return pl.pallas_call(
        functools.partial(ff_grad_body, ndp, nseq, spans, owned, len(waits)),
        name="feed_forward_gradients",
        grid_spec=pltpu.PrefetchScalarGridSpec(
            num_scalar_prefetch=1,
            grid=(1,),
            in_specs=[in_place] * (len(blocks) + len(waits) + len(sides) + 1),
            out_specs=whole_spec(*pack),
            scratch_shapes=[
                pltpu.VMEM((rows, width), BF16),
                pltpu.VMEM((rows, width), BF16),
                pltpu.VMEM((rows, wide), BF16),
                pltpu.VMEM((rows, wide), BF16),
                pltpu.VMEM((rows, wide), BF16),
                pltpu.SemaphoreType.DMA((count,)),
            ],
        ),
        out_shape=jax.ShapeDtypeStruct(pack, BF16),
        compiler_params=kernel_params(48),
        cost_estimate=NO_COST,
    )(place, *blocks, *waits, *sides, grad_blocks)


def unpack_ff_body(ndp, own_rows, down_rows, pack_ref, gate_w_ref, up_w_ref, down_ref, gate_ref, up_ref, gain_ref):
    nseq = pack_ref.shape[0]
    slice_ff, width = down_ref.shape
    wide = -(-slice_ff // 128) * 128
    low = lax.broadcasted_iota(jnp.int32, (own_rows, 128), 1) < 64
    for seq in range(nseq):
        keep = min(down_rows, slice_ff - seq * down_rows)
        for tile in range(width // 128):
            if keep > 0:
                part = pack_ref[seq, tile * down_rows : (tile + 1) * down_rows].astype(F32)
                down_ref[seq * down_rows : seq * down_rows + keep, tile * 128 : (tile + 1) * 128] = part[:keep]
    for seq in range(gate_ref.shape[0] // own_rows):
        span = slice(seq * own_rows, (seq + 1) * own_rows)
        total = jnp.zeros((own_rows, 1), F32)
        for which, (out_ref, w_ref) in enumerate(((gate_ref, gate_w_ref), (up_ref, up_w_ref))):

            def tile_of(dp, tile):
                first = down_rows * width // 128 + ((2 * dp + which) * (wide // 128) + tile) * own_rows
                return pack_ref[seq, first : first + own_rows].astype(F32)

            whole_tiles = slice_ff // 128
            for dp in range(0, ndp, 2):
                first = dp * slice_ff // 128
                parts = [tile_of(dp, t) for t in range(whole_tiles)]
                halves = [pltpu.roll(tile_of(dp + 1, t), 64, 1) for t in range(whole_tiles + 1)]
                parts.append(jnp.where(low, tile_of(dp, whole_tiles), halves[0]))
                parts += [jnp.where(low, halves[t], halves[t + 1]) for t in range(whole_tiles)]
                for t, part in enumerate(parts):
                    cols = slice((first + t) * 128, (first + t + 1) * 128)
                    out_ref[span, cols] = part
                    total += jnp.sum(part * w_ref[span, cols].astype(F32), axis=1, keepdims=True)
        gain_ref[span] = jnp.broadcast_to(total, (own_rows, 128))


def unpack_ff(pack, w_gate, w_up, slice_ff, width, own_rows, down_rows):
    shard, ff = w_gate.shape
    full = jax.ShapeDtypeStruct((shard, ff), F32)
    return pl.pallas_call(
        functools.partial(unpack_ff_body, ff // slice_ff, own_rows, down_rows),
        name="unpack_feed_forward",
        grid=(1,),
        in_specs=[whole_spec(*pack.shape), whole_spec(shard, ff), whole_spec(shard, ff)],
        out_specs=[whole_spec(slice_ff, width), whole_spec(shard, ff), whole_spec(shard, ff), whole_spec(shard, 128)],
        out_shape=[
            jax.ShapeDtypeStruct((slice_ff, width), F32), full, full, jax.ShapeDtypeStruct((shard, 128), F32),
        ],
        compiler_params=kernel_params(40),
        cost_estimate=NO_COST,
    )(pack, w_gate, w_up)


def unpack_attention_body(
    sections, pack_ref, query_w_ref, latent_w_ref, query_ref, key_ref, value_ref, out_ref, latent_ref, gain_ref
):
    nz, _, rows, _ = pack_ref.shape
    step = 32
    for core in range(2):
        first = 0
        for section, target in zip(sections[:4], (query_ref, key_ref, value_ref, out_ref)):
            for row in range(0, section, step):
                place = first + row
                part = pack_ref[place // rows, core, place % rows : place % rows + step].astype(F32)
                target[core * section + row : core * section + row + step] = part
            first += section
        for row in range(0, sections[4], step):
            place = first + row
            part = pack_ref[place // rows, core, place % rows : place % rows + step].astype(F32)
            width = latent_ref.shape[1]
            for i in range(part.shape[1] // width):
                base = core * sections[0] + i * sections[4] + row
                latent_ref[base : base + step] = part[:, i * width : (i + 1) * width]
    total = jnp.sum(query_w_ref[...].astype(F32) * query_ref[...], axis=1, keepdims=True)
    total += jnp.sum(latent_w_ref[...].astype(F32) * latent_ref[...], axis=1, keepdims=True)
    gain_ref[...] = jnp.broadcast_to(total, gain_ref.shape)


def unpack_attention(pack, w_query, w_latent, sections):
    shard, width = w_query.shape
    lat_width = w_latent.shape[1]
    shapes = [
        (shard, width), (2 * sections[1], width), (2 * sections[2], width), (2 * sections[3], width),
        (shard, lat_width), (shard, 128),
    ]
    return pl.pallas_call(
        functools.partial(unpack_attention_body, sections),
        name="unpack_attention",
        grid=(1,),
        in_specs=[whole_spec(*pack.shape), whole_spec(shard, width), whole_spec(shard, lat_width)],
        out_specs=[whole_spec(*shape) for shape in shapes],
        out_shape=[jax.ShapeDtypeStruct(shape, F32) for shape in shapes],
        compiler_params=kernel_params(24),
        cost_estimate=NO_COST,
    )(pack, w_query, w_latent)


def inverse_rms(values):
    return lax.rsqrt(jnp.mean(values * values, axis=-1, keepdims=True) + NORM_EPS)


def norm_pull(values, inverse, gain, grads):
    scaled = gain * grads
    return inverse * scaled - values * (inverse**3) * jnp.mean(scaled * values, axis=-1, keepdims=True)


def my_half(shard):
    half = shard.shape[0] // 2
    return lax.dynamic_slice_in_dim(shard, lax.axis_index("core") * half, half, 0)


def swap_core(x):
    return lax.ppermute(x, "core", [(0, 1), (1, 0)])


def partner(x, step):
    return lax.ppermute(x, DP, [(i, i ^ step) for i in range(lax.axis_size(DP))])


def from_behind(x, step):
    nz = lax.axis_size("z")
    return lax.ppermute(x, "z", [(i, (i + step) % nz) for i in range(nz)])


def from_ahead(x, step):
    nz = lax.axis_size("z")
    return lax.ppermute(x, "z", [((i + step) % nz, i) for i in range(nz)])


def gather_dp(x):
    return [x] + [partner(x, step) for step in range(1, lax.axis_size(DP))]


def scatter_dp(parts):
    total = parts[0].astype(F32)
    for step in range(1, len(parts)):
        total = total + partner(parts[step].astype(BF16), step).astype(F32)
    return total


def together(*arrays):
    return lax.optimization_barrier(arrays)


def per_device(
    tokens, norm1_gain, w_query, w_latent, w_key_up, w_value_up, w_out, norm2_gain,
    w_gate, w_up, w_down, out_grad, seq_lengths,
):
    ndp = lax.axis_size(DP)
    nz = lax.axis_size("z")
    nseq = 2 * nz
    pieces, strip, width = tokens.shape[1:]
    rows = pieces * strip
    lat_width = GROUPS * LATENT
    my_z, my_core, my_dp = lax.axis_index("z"), lax.axis_index("core"), lax.axis_index(DP)
    shard = norm1_gain.shape[0]
    slice_ff = w_down.shape[0]
    wide_ff = -(-slice_ff // 128) * 128
    half = shard // 2

    gains = jnp.pad(jnp.concatenate([norm1_gain, norm2_gain])[None, :], ((0, 15), (0, lat_width - 2 * shard)))
    own_head = jnp.concatenate([my_half(w_latent), gains], axis=0)
    place = jnp.stack([my_core, my_dp, my_z]).astype(jnp.int32)
    by_step = gather_dp(own_head)
    pack = lax.all_gather(
        jnp.concatenate(
            [
                my_half(w_query), my_half(w_key_up), my_half(w_value_up), my_half(w_out),
                out_grad[0].reshape(rows, width),
            ],
            axis=0,
        ),
        CHIP,
        axis=0,
    )

    table, tables = positions_of(place, seq_lengths, pieces, nz, strip)

    tok_rows = tokens[0].reshape(rows, width)
    normed, latent, gains, latent_w = front(place, tok_rows, by_step, swap_core(jnp.stack(by_step)))
    latent = latent.reshape(pieces, strip, lat_width)
    gain_one, gain_two = gains[0:1], gains[8:9]
    tok = tok_rows.astype(F32)
    inv_one = inverse_rms(tok)
    behind = [from_behind(latent, step) for step in range(1, nz)]
    pack, cut_ff, *behind = together(pack, cut_columns(place, w_gate, w_up, ndp, half), *behind)
    sliced = lax.all_to_all(cut_ff, DP, 0, 0, tiled=True)
    up_half = w_key_up.shape[0] // 2
    cuts = [0, half, half + up_half, half + 2 * up_half, 2 * half + 2 * up_half]
    pack, normed_in = together(pack, normed)
    normed_stream = lax.all_gather(normed_in.reshape(pieces, strip, width), SEQ, axis=0)
    query_w, key_w, value_w, out_w = (pack[:, a:b].reshape(-1, width) for a, b in zip(cuts[:-1], cuts[1:]))
    queries = mm(normed, query_w).astype(BF16)
    core_lat = [latent, *behind]
    latents = core_lat + [swap_core(x) for x in core_lat]

    grad_rows = out_grad[0].reshape(rows, width)
    grad_blocks, lead = pack, pack.shape[1] - rows
    cut = pieces // 2
    chunks = [(cut, pieces - cut), (0, cut)]

    def rows_of(x, chunk):
        return x[chunk[0] * strip : (chunk[0] + chunk[1]) * strip]

    def pieces_of(x, chunk):
        return x[chunk[0] : chunk[0] + chunk[1]]

    kept = []
    for chunk in chunks:
        absorbed, mixed, lse, heads_out = attention_forward(
            *chunk, tables, pieces_of(table, chunk), latents, rows_of(queries, chunk), key_w, value_w,
            [kept[0][6][0], sliced] if kept else [],
        )
        if kept:
            heads_out, *fresh = together(heads_out, *kept[0][6])
            kept[0][6][:] = fresh
        resid = rows_of(tok, chunk) + mm(heads_out, out_w)
        inv_two = inverse_rms(resid)
        normed_two = (resid * inv_two * gain_two).astype(BF16)
        kept.append((absorbed, mixed, lse, heads_out, resid, inv_two, gather_dp(normed_two)))


    sliced_other = swap_core(sliced)
    ff_sides = []
    ff_parts = []
    for chunk, state in zip(chunks, kept):
        blocks = state[6]
        out = feed_forward(
            place, lead + chunk[0] * strip, blocks, grad_blocks, sliced, sliced_other, w_down,
            [ff_parts[0][0]] if ff_parts else [kept[1][6][0]],
        )
        ff_sides.append((blocks, out[:3]))
        ff_parts.append(out[3:])
    received = [[partner(x, step) for step, x in enumerate(parts) if step] for parts in ff_parts]
    d_resids = []
    for chunk, state, parts, others in zip(chunks, kept, ff_parts, received):
        resid, inv_two = state[4:6]
        d_normed_two = sum((x.astype(F32) for x in others), parts[0].astype(F32))
        d_resids.append(
            rows_of(grad_rows, chunk).astype(F32) + norm_pull(resid, inv_two, gain_two, d_normed_two)
        )

    down_rows = -(-slice_ff // (16 * nseq)) * 16
    own_rows = -(-shard // (16 * nseq)) * 16
    ff_pack = ff_gradients(
        place,
        [(lead + chunk[0] * strip, chunk[1] * strip) for chunk in chunks],
        [x for blocks, _ in ff_sides for x in blocks],
        [x for _, sides in ff_sides for x in sides],
        grad_blocks,
        nseq,
        (down_rows, own_rows),
        [],
    )
    down_wide = jnp.pad(w_down, ((0, wide_ff - slice_ff), (0, 0)))
    ff_whole = ff_pack

    ff_pack = lax.psum_scatter(ff_pack, SEQ, scatter_dimension=0, tiled=True)[0]

    order_of = [chunks.index((0, cut)), chunks.index((cut, pieces - cut))]
    d_resid = jnp.concatenate([d_resids[i] for i in order_of])
    resid = jnp.concatenate([kept[i][4] for i in order_of])
    heads_out = jnp.concatenate([kept[i][3] for i in order_of])
    d_resid_round = d_resid.astype(BF16)
    d_heads = mm_nt(d_resid_round, out_w).astype(BF16)
    absorbed, mixed, lse = ([kept[i][which] for i in order_of] for which in range(3))
    d_queries, d_lat, part_mine, part_theirs = attention_backward(
        tables, place, latents, table, queries, key_w, value_w, normed, heads_out, d_resid_round, normed_stream,
        absorbed, mixed, lse, d_heads, ndp, [ff_whole],
    )
    ff_pack, part_theirs = together(ff_pack, part_theirs)
    part_other = swap_core(part_theirs)
    chip_parts = [
        (part_mine[i].astype(F32) + part_other[i].astype(F32)).astype(BF16) for i in range(ndp)
    ]
    d_lat, *chip_parts = together(d_lat, *chip_parts)
    out_sides = together(chip_parts[0], *[sides[0] for _, sides in ff_sides])
    chip_parts[0] = out_sides[0]
    out_parts = [mm(x, down_wide).astype(BF16) for x in out_sides[1:]]
    core_sum = d_lat[:nz].astype(F32) + swap_core(d_lat[nz:]).astype(F32)
    send = core_sum.astype(BF16)
    d_latent = core_sum[0]
    for step in range(1, nz):
        d_latent = d_latent + from_ahead(send[step], step).astype(F32)
    d_latent = d_latent.astype(BF16).reshape(rows, lat_width)
    down_lines = down_rows * width // 128
    swap = ff_pack[down_lines:].reshape(ndp, -1, 128)
    swap = lax.all_to_all(swap, DP, 0, 0, tiled=True)
    ff_pack = jnp.concatenate([ff_pack[:down_lines], swap.reshape(-1, 128)], axis=0)
    ff_gathered = lax.all_gather(ff_pack, SEQ, axis=0)
    d_normed = mm_nt(d_queries, query_w) + mm_nt(d_latent, latent_w)
    tokens_grad = (d_resid + norm_pull(tok, inv_one, gain_one, d_normed)).astype(BF16)
    block = []
    for i in range(ndp):
        parts = [x[i * chunk[1] * strip : (i + 1) * chunk[1] * strip] for x, chunk in zip(out_parts, chunks)]
        block.append(jnp.concatenate([parts[j] for j in order_of]))
    layer_out = (resid + scatter_dp(block)).astype(BF16)

    grad_pack = scatter_dp(chip_parts).astype(BF16)
    own, ff_gathered = together(grad_pack, ff_gathered)
    own = own.reshape(nz, -1, width)
    down_out, gate_out, up_out, gain_two_sum = unpack_ff(
        ff_gathered, w_gate, w_up, slice_ff, width, own_rows, down_rows
    )
    own = lax.psum_scatter(own, "z", scatter_dimension=0, tiled=True)
    own, gain_two_sum = together(own[0], gain_two_sum)
    own = lax.all_gather(own, SEQ, axis=0).reshape(nz, 2, -1, width)
    lat_rows = half * lat_width // width
    sections = (half, up_half, up_half, half, lat_rows)
    if own.shape[2] % 32 == 0:
        query_out, key_out, value_out, out_out, latent_out, gain_one_sum = unpack_attention(
            own, w_query, w_latent, sections
        )
    else:
        own = own.transpose(1, 0, 2, 3).reshape(2, -1, width).astype(F32)
        query_out, key_out, value_out, out_out, latent_out = (
            own[:, cut : cut + count].reshape(-1, width) for cut, count in zip([*cuts[:-1], cuts[-1]], sections)
        )
        fold = width // lat_width
        latent_out = latent_out.reshape(2, lat_rows, fold, lat_width).transpose(0, 2, 1, 3).reshape(shard, lat_width)
        gain_one_sum = jnp.sum(w_query.astype(F32) * query_out, axis=1, keepdims=True)
        gain_one_sum += jnp.sum(w_latent.astype(F32) * latent_out, axis=1, keepdims=True)

    gain_one_out = gain_one_sum[:, 0] / norm1_gain.astype(F32)
    gain_two_out = gain_two_sum[:, 0] / norm2_gain.astype(F32)

    shape = (1, pieces, strip, width)
    return (
        layer_out.reshape(shape), tokens_grad.reshape(shape), gain_one_out, query_out, latent_out, key_out,
        value_out, out_out, gain_two_out, gate_out, up_out, down_out,
    )


def solution(mesh):
    sizes = mesh.shape
    grid = Mesh(mesh.devices.reshape(sizes["dp"], sizes["seq"] // 2, 2), ("dp", "z", "core"))
    stream = P("dp", None, SEQ, None)
    vector, matrix = P("dp"), P("dp", None)
    in_specs = (
        stream, vector, matrix, matrix, matrix, matrix, matrix, vector, matrix, matrix, matrix, stream, matrix,
    )
    out_specs = (
        stream, stream, vector, matrix, matrix, matrix, matrix, matrix, vector, matrix, matrix, matrix,
    )
    return jax.shard_map(per_device, mesh=grid, in_specs=in_specs, out_specs=out_specs, check_vma=False)
```
